128 devices in a mesh: series: 32 (over z, y, core), mp: 4 (over x).
Axes of the slice: x: 4, y: 4, z: 4, core: 2. Of those that a mesh axis runs over, the one named last changes fastest.
Arguments:
- series_in: bfloat16 [512, 256, 768], P('series'), may hold values from -6 to 6
- norm_gain: float32 [768], replicated, may hold values from 0.5 to 1.5
- w_time: bfloat16 [768, 12, 192], P(None, 'mp'), may hold values from -0.375 to 0.375
- w_group: bfloat16 [768, 12, 192], P(None, 'mp'), may hold values from -0.375 to 0.375
- w_gate: bfloat16 [768, 768], P(None, 'mp'), may hold values from -0.4375 to 0.4375
- w_out: bfloat16 [768, 768], P('mp'), may hold values from -0.4375 to 0.4375
- group_of: int32 [512], replicated, may hold values from 0 to 14, as said below
Outputs:
- block_out: bfloat16 [512, 256, 768], P('series', None, 'mp')
The draws below stay inside these ranges and needn't reach their ends.
Inputs may be any that keep to these rules, and one draw needn't show every extreme that they name: `group_of`: groups are numbered from 0 without gaps; each holds 8 to 64 series, one group exactly 8 and one exactly 64; members are spread over the series at random.
All inputs are finite; a program needn't handle non-finite values.
Results may differ from the reference program's by a relative error of at most 0.015.
Values may be sent and summed in bfloat16 or wider, within the bound.
No kernel may reach another device: no remote copies, remote signals or barrier semaphores. Data moves between devices by JAX's collectives and lax.ppermute only.
A program may use at most 128 MiB of HBM per device.

```python
import jax
import jax.numpy as jnp
from jax import lax

D = 768
HEADS = 12
HD = 64
SER_DEV = 16
P_SIZE = 256
GROUP_MIN = 8
GROUP_MAX = 64
SERIES = 512
HEADS_DEV = 3
N_SERIES = 32
N_MP = 4


def draw_group_of(key, part):
    key_sizes = jax.random.fold_in(key, 11)
    key_order = jax.random.fold_in(key, 23)
    mean_size = (GROUP_MIN + GROUP_MAX) // 2
    rest_series = SERIES - GROUP_MIN - GROUP_MAX
    other_count = (rest_series + mean_size - 1) // mean_size
    slot_index = jnp.arange(other_count)
    base_sizes = rest_series // other_count + (slot_index < rest_series % other_count).astype(jnp.int32)
    pair_count = other_count // 2
    if pair_count > 0:
        donors = base_sizes[0:2 * pair_count:2]
        takers = base_sizes[1:2 * pair_count:2]
        limits = jnp.minimum(donors - GROUP_MIN, GROUP_MAX - takers)
        moved = jax.random.randint(key_sizes, (pair_count,), 0, limits + 1)
        base_sizes = base_sizes.at[0:2 * pair_count:2].add(-moved)
        base_sizes = base_sizes.at[1:2 * pair_count:2].add(moved)
    group_sizes = jnp.concatenate([jnp.array([GROUP_MIN, GROUP_MAX], jnp.int32), base_sizes.astype(jnp.int32)])
    group_ends = jnp.cumsum(group_sizes)
    position = jnp.arange(SERIES)
    group_index = jnp.sum((position[:, None] >= group_ends[None, :]).astype(jnp.int32), axis=1)
    shuffle = jax.random.permutation(key_order, SERIES)
    return group_index[jnp.argsort(shuffle)].astype(jnp.int32)


def shard_levels(stream_key, shape, cuts, least, top_value):
    def one(axis_at, shards_of):
        draws = jax.random.uniform(jax.random.fold_in(jax.random.fold_in(stream_key, 6), axis_at), (shards_of,), jnp.float32, least / len(cuts), top_value / len(cuts))
        return jnp.repeat(jnp.exp(draws), shape[axis_at] // shards_of).reshape((-1,) + (1,) * (len(shape) - axis_at - 1))

    factor_of = one(*cuts[0])
    for cut in cuts[1:]:
        factor_of = factor_of * one(*cut)
    return factor_of


def noise(key, extent, deviation, limit, pieces=(), dtype=jnp.bfloat16):
    entries = jax.random.normal(key, extent, jnp.float32) * deviation
    if len(pieces) > 0:
        entries = shard_levels(key, extent, pieces, -0.22, 0.18) * entries
    return jnp.clip(entries, min=-limit, max=limit).astype(dtype)


def setup_inputs(seed: int = 0) -> dict:
    splits = jax.random.split(jax.random.key(seed), 8)
    series_in = noise(splits[0], (SERIES, P_SIZE, D), 1.0, 6.0, ((0, 32),))
    norm_gain = jnp.clip(1.0 + 0.1 * jax.random.normal(splits[1], (D,), jnp.float32), 0.5, 1.5)
    w_time = noise(splits[2], (D, HEADS, 3 * HD), (D // 3) ** -0.5, 0.375, ((1, 4),))
    w_group = noise(splits[3], (D, HEADS, 3 * HD), (D // 3) ** -0.5, 0.375, ((1, 4),))
    w_gate = noise(splits[4], (D, HEADS * HD), (D // 4) ** -0.5, 0.4375, ((1, 4),))
    w_out = noise(splits[5], (HEADS * HD, D), (HEADS * HD // 4) ** -0.5, 0.4375, ((0, 4),))
    group_of = draw_group_of(jax.random.fold_in(splits[7], 71), 0)
    return {"series_in": series_in, "norm_gain": norm_gain, "w_time": w_time, "w_group": w_group, "w_gate": w_gate, "w_out": w_out, "group_of": group_of}


def rms_norm(series_in, norm_gain):
    values_f = series_in.astype(jnp.float32)
    mean_sq = lax.optimization_barrier(jnp.mean(values_f * values_f, axis=-1, keepdims=True))
    return (values_f * lax.rsqrt(mean_sq + 1e-06) * norm_gain.astype(jnp.float32)).astype(jnp.bfloat16)

def time_block(block_qkv):
    queries = block_qkv[:, :, :, 0].astype(jnp.float32)
    keys_in = block_qkv[:, :, :, 1].astype(jnp.float32)
    values_in = block_qkv[:, :, :, 2].astype(jnp.float32)
    scores = jnp.einsum('bphd,bqhd->bhpq', queries, keys_in) * HD ** (-0.5)
    weights = lax.optimization_barrier(jax.nn.softmax(scores, axis=-1).astype(jnp.bfloat16))
    return jnp.einsum('bhpq,bqhd->bphd', weights.astype(jnp.float32), values_in).astype(jnp.bfloat16)

def group_patch(patch_qkv, same_group):
    queries = patch_qkv[:, :, 0].astype(jnp.float32)
    keys_in = patch_qkv[:, :, 1].astype(jnp.float32)
    values_in = patch_qkv[:, :, 2].astype(jnp.float32)
    scores = jnp.einsum('ihd,jhd->hij', queries, keys_in) * HD ** (-0.5)
    scores = jnp.where(same_group[None], scores, -1e+30)
    weights = lax.optimization_barrier(jax.nn.softmax(scores, axis=-1).astype(jnp.bfloat16))
    return jnp.einsum('hij,jhd->ihd', weights.astype(jnp.float32), values_in).astype(jnp.bfloat16)

def reference(series_in, norm_gain, w_time, w_group, w_gate, w_out, group_of):
    normed = rms_norm(series_in, norm_gain)
    flat_rows = normed.reshape(SERIES * P_SIZE, D)
    time_qkv = jnp.dot(flat_rows, w_time.reshape(D, -1), preferred_element_type=jnp.float32).astype(jnp.bfloat16)
    time_qkv = time_qkv.reshape(N_SERIES, SER_DEV, P_SIZE, HEADS, 3, HD)
    time_out = lax.map(time_block, time_qkv).reshape(SERIES * P_SIZE, HEADS * HD)
    group_qkv = jnp.dot(flat_rows, w_group.reshape(D, -1), preferred_element_type=jnp.float32).astype(jnp.bfloat16)
    group_qkv = group_qkv.reshape(SERIES, P_SIZE, HEADS, 3, HD)
    same_group = group_of[:, None] == group_of[None, :]
    group_out = lax.map(lambda patch_qkv: group_patch(patch_qkv, same_group), jnp.moveaxis(group_qkv, 1, 0))
    group_out = jnp.moveaxis(group_out, 0, 1).reshape(SERIES * P_SIZE, HEADS * HD)
    gate_value = jax.nn.sigmoid(jnp.dot(flat_rows, w_gate, preferred_element_type=jnp.float32))
    merged = (time_out.astype(jnp.float32) + gate_value * group_out.astype(jnp.float32)).astype(jnp.bfloat16)
    width_dev = HEADS_DEV * HD
    total_sum = jnp.zeros((SERIES * P_SIZE, D), jnp.float32)
    for member in range(N_MP):
        head_term = jnp.dot(merged[:, member * width_dev:(member + 1) * width_dev], w_out[member * width_dev:(member + 1) * width_dev], preferred_element_type=jnp.float32)
        total_sum = total_sum + head_term.astype(jnp.bfloat16).astype(jnp.float32)
    return total_sum.astype(jnp.bfloat16).reshape(SERIES, P_SIZE, D)
```

```python
from functools import partial

import jax
import jax.numpy as jnp
from jax import lax
from jax.experimental import pallas as pl
from jax.experimental.pallas import tpu as pltpu
from jax.sharding import Mesh
from jax.sharding import PartitionSpec as P

BF = jnp.bfloat16
F32 = jnp.float32
SERIES_AXES = ("sc", "core")
BIG = 2.0**50


def nt(a, b):
    return lax.dot_general(a, b, (((1,), (1,)), ((), ())), preferred_element_type=F32)


def nn(a, b):
    return lax.dot_general(a, b, (((1,), (0,)), ((), ())), preferred_element_type=F32)


def tn(a, b):
    return lax.dot_general(a, b, (((0,), (0,)), ((), ())), preferred_element_type=F32)


def params(mib=56):
    return pltpu.CompilerParams(vmem_limit_bytes=mib << 20)


def normed_rows(x, gain):
    xf = x.astype(F32)
    mean_sq = jnp.mean(xf * xf, axis=-1, keepdims=True)
    return (xf * lax.rsqrt(mean_sq + 1e-06) * gain).astype(BF)


def pack_kernel(me_ref, x_ref, o_ref, tmp):
    ser, rows, _ = x_ref.shape
    blocks = tmp.shape[0]
    for i in range(ser):
        values = x_ref[i].astype(F32)
        for c in range(blocks):
            tmp[c, pl.ds(i, rows, stride=ser), :] = values[:, c * 128 : (c + 1) * 128]
    for c in range(blocks):
        o_ref[:, c * 128 : (c + 1) * 128] = tmp[c].astype(BF)


def pack(series_in, me, half, n_ser):
    ser, patches, width = series_in.shape
    n_mp = patches // (2 * n_ser)
    return pl.pallas_call(
        pack_kernel,
        out_shape=jax.ShapeDtypeStruct((n_ser * ser, width), BF),
        grid_spec=pltpu.PrefetchScalarGridSpec(
            num_scalar_prefetch=1,
            grid=(1,),
            in_specs=[
                pl.BlockSpec((ser, n_ser, width), lambda g, me: (0, half * n_mp + me[0], 0))
            ],
            out_specs=pl.BlockSpec((n_ser * ser, width), lambda g, me: (0, 0)),
            scratch_shapes=[pltpu.VMEM((width // 128, n_ser * ser, 128), F32)],
        ),
        compiler_params=params(),
        name="pack",
    )(me, series_in)


def time_kernel(x_ref, gain_ref, w_ref, o_ref, w_qv, w_k):
    hd = 64
    heads = w_ref.shape[0] // (3 * hd)

    @pl.when(pl.program_id(0) == 0)
    def _():
        for h in range(heads):
            base = h * 3 * hd
            w_qv[h * hd : (h + 1) * hd] = w_ref[base : base + hd]
            w_k[h * hd : (h + 1) * hd] = w_ref[base + hd : base + 2 * hd]
            w_qv[(heads + h) * hd : (heads + h + 1) * hd] = w_ref[base + 2 * hd : base + 3 * hd]

    rows = x_ref.shape[1]
    normed = normed_rows(x_ref[0], gain_ref[...])
    qv_t = nt(w_qv[...], normed)
    keys = nt(normed, w_k[...]).astype(BF)
    q_t = (qv_t[: heads * hd] * 0.125).astype(BF)
    v_t = qv_t[heads * hd :].astype(BF)
    zeros = jnp.zeros((hd, rows), BF)
    ones = jnp.ones((16, rows), BF)
    for h in range(heads):
        block = h // 2
        q_h = q_t[h * hd : (h + 1) * hd]
        if 2 * block + 1 < heads:
            q_h = jnp.concatenate([q_h, zeros] if h % 2 == 0 else [zeros, q_h], axis=0)
            k_h = keys[:, block * 128 : block * 128 + 128]
        else:
            k_h = keys[:, block * 128 : block * 128 + hd]
        scores = nn(k_h, q_h)
        top = jnp.max(scores, axis=0, keepdims=True)
        weights = jnp.exp(scores - top).astype(BF)
        out = nn(jnp.concatenate([v_t[h * hd : (h + 1) * hd], ones], axis=0), weights)
        o_ref[0, h * hd : (h + 1) * hd, :] = (out[:hd] / out[hd : hd + 1]).astype(BF)


def time_part(series_in, gain, w_time_t):
    ser, patches, width = series_in.shape
    chan = w_time_t.shape[0] // 3
    return pl.pallas_call(
        time_kernel,
        out_shape=jax.ShapeDtypeStruct((ser, chan, patches), BF),
        grid=(ser,),
        in_specs=[
            pl.BlockSpec((1, patches, width), lambda i: (i, 0, 0)),
            pl.BlockSpec((1, width), lambda i: (0, 0)),
            pl.BlockSpec((3 * chan, width), lambda i: (0, 0)),
        ],
        out_specs=pl.BlockSpec((1, chan, patches), lambda i: (i, 0, 0)),
        scratch_shapes=[pltpu.VMEM((2 * chan, width), BF), pltpu.VMEM((chan, width), BF)],
        compiler_params=params(),
        name="time",
    )(series_in, gain, w_time_t)


def project_kernel(t_ref, w_ref, o_ref):
    members, ser, chan, patches = t_ref.shape
    w_t = w_ref[...].reshape(members * chan, -1).T
    cols = w_t.shape[0] // members
    for i in range(ser):
        rows = t_ref[:, i].reshape(members * chan, patches)
        out = nn(w_t, rows).astype(BF)
        for m in range(members):
            o_ref[m, i] = out[m * cols : (m + 1) * cols]


def project(time_rows, w_out):
    return pl.pallas_call(
        project_kernel,
        out_shape=jax.ShapeDtypeStruct(time_rows.shape, BF),
        compiler_params=params(),
        name="project",
    )(time_rows, w_out)


def group_kernel(x_ref, gain_ref, wg_ref, wgate_ref, wout_ref, gcol_ref, grow_ref, o_ref,
                 w_q, w_k, w_v, kmat, qmat, vmat, gated):
    hd = 64
    members, per, width = wg_ref.shape
    heads_m = per // (3 * hd)
    heads = members * heads_m
    n = x_ref.shape[0]
    for h in range(heads):
        m, base = h // heads_m, (h % heads_m) * 3 * hd
        w_q[h * hd : (h + 1) * hd] = wg_ref[m, base : base + hd]
        w_k[h * hd : (h + 1) * hd] = wg_ref[m, base + hd : base + 2 * hd]
        w_v[h * hd : (h + 1) * hd] = wg_ref[m, base + 2 * hd : base + 3 * hd]
    normed = normed_rows(x_ref[...], gain_ref[...])
    keys = nt(normed, w_k[...]).astype(BF)
    for b in range(heads // 2):
        kmat[b] = keys[:, b * 128 : (b + 1) * 128]
    qmat[...] = (nt(w_q[...], normed) * 0.125).astype(BF).reshape(qmat.shape)
    vmat[...] = nt(w_v[...], normed).astype(BF).reshape(vmat.shape)
    lanes = lax.broadcasted_iota(jnp.int32, (n, 128), 1)
    k_mask = jnp.where(gcol_ref[...] == lanes, 0.0, -BIG).astype(BF)
    subl = lax.broadcasted_iota(jnp.int32, (128, n), 0)
    q_mask = jnp.where(grow_ref[...] == subl, BIG, 0.0).astype(BF)
    zeros = jnp.zeros((hd, n), BF)
    ones = jnp.ones((16, n), BF)

    def pair(b, carry):
        k_b = jnp.concatenate([kmat[b], k_mask], axis=1)
        for e in range(2):
            q_e = qmat[2 * b + e]
            parts = [q_e, zeros] if e == 0 else [zeros, q_e]
            q_e = jnp.concatenate(parts + [q_mask], axis=0)
            v_e = jnp.concatenate([vmat[2 * b + e], ones], axis=0)
            for c in range(n // 256):
                scores = nn(k_b, q_e[:, c * 256 : (c + 1) * 256])
                top = jnp.max(scores, axis=0, keepdims=True)
                weights = jnp.exp(scores - top).astype(BF)
                out = nn(v_e, weights)
                gated[2 * b + e, :, c * 256 : (c + 1) * 256] = (
                    out[:hd] / out[hd : hd + 1]
                ).astype(BF)
        return carry

    lax.fori_loop(0, heads // 2, pair, 0)
    gate = jax.nn.sigmoid(nt(wgate_ref[...].reshape(heads * hd, width), normed))
    rows = (gate * gated[...].reshape(heads * hd, n).astype(F32)).astype(BF)
    out = tn(rows, wout_ref[...].reshape(heads * hd, width))
    cols = width // members
    for m in range(members):
        part = out[:, m * cols : (m + 1) * cols].reshape(n // 16, 16, cols)
        low, high = part[:, :8], part[:, 8:]
        o_ref[m] = jnp.concatenate(
            [low[:, :, :128], high[:, :, :128], low[:, :, 128:], high[:, :, 128:]], axis=-1
        ).astype(BF)


def group_part(rows, gain, w_group, w_gate, w_out, group_col, group_row):
    n, width = rows.shape
    members, chan, _ = w_gate.shape
    heads = members * chan // 64
    return pl.pallas_call(
        group_kernel,
        out_shape=jax.ShapeDtypeStruct((members, n // 16, 8, 2 * width // members), BF),
        scratch_shapes=[
            pltpu.VMEM((heads * 64, width), BF),
            pltpu.VMEM((heads * 64, width), BF),
            pltpu.VMEM((heads * 64, width), BF),
            pltpu.VMEM((heads // 2, n, 128), BF),
            pltpu.VMEM((heads, 64, n), BF),
            pltpu.VMEM((heads, 64, n), BF),
            pltpu.VMEM((heads, 64, n), BF),
        ],
        compiler_params=params(),
        name="group",
    )(rows, gain, w_group, w_gate, w_out, group_col, group_row)


def join_kernel(t_ref, g0_ref, g1_ref, o_ref, tmp):
    i = pl.program_id(0)
    for j, g_ref in enumerate((g0_ref, g1_ref)):
        @pl.when(i == 0)
        def _():
            for c in range(tmp.shape[1]):
                tmp[j, c] = g_ref[:, c * 128 : (c + 1) * 128].astype(F32)

    for j in range(2):
        rows = [tmp[j, c, pl.ds(i, 128, stride=8), :].T for c in range(tmp.shape[1])]
        lanes = slice(j * 128, (j + 1) * 128)
        for e in range(2):
            top = t_ref[e, 0, :128, lanes].astype(F32) + rows[e]
            low = t_ref[e, 0, 128:, lanes].astype(F32) + rows[2][e * 64 : (e + 1) * 64]
            o_ref[e, 0, :128, lanes] = top.astype(BF)
            o_ref[e, 0, 128:, lanes] = low.astype(BF)


def join(time_cols, group0, group1):
    ser, cols, patches = time_cols.shape
    spec = pl.BlockSpec((2, 1, cols, patches), lambda i: (0, i, 0, 0))
    whole = pl.BlockSpec(group0.shape, lambda i: (0, 0))
    return pl.pallas_call(
        join_kernel,
        out_shape=jax.ShapeDtypeStruct((2, ser // 2, cols, patches), BF),
        grid=(ser // 2,),
        in_specs=[spec, whole, whole],
        out_specs=spec,
        scratch_shapes=[pltpu.VMEM((2, group0.shape[1] // 128, group0.shape[0], 128), F32)],
        compiler_params=params(),
        name="join",
    )(time_cols.reshape(2, ser // 2, cols, patches), group0, group1)


def around(shard):
    members = lax.axis_size("mp")
    step = lambda value, by: lax.ppermute(
        value, "mp", [(i, (i + by) % members) for i in range(members)]
    )
    core = lax.axis_index("core")
    half = shard.shape[0] // 2
    mine = lax.dynamic_slice_in_dim(shard, core * half, half, 0)
    left = step(mine, 1)
    right = step(mine, members - 1)
    quarter = half // 2
    far_a = step(left[:quarter], 1)
    far_b = step(right[quarter:], members - 1)
    far = jnp.concatenate([far_a, far_b], axis=0)
    got = jnp.stack([left, right, far])
    other = lax.ppermute(got, "core", [(0, 1), (1, 0)])
    first = core == 0
    full = jnp.concatenate(
        [jnp.where(first, got, other), jnp.where(first, other, got)], axis=1
    )
    return jnp.concatenate([shard[None], full], axis=0)


def per_device(series_in, norm_gain, w_time, w_group, w_gate, w_out, group_of):
    ser, patches, width = series_in.shape
    members = lax.axis_size("mp")
    n_ser = lax.axis_size("sc") * lax.axis_size("core")
    chan = w_gate.shape[1]
    me = lax.axis_index("mp").reshape(1)
    gain = norm_gain.reshape(1, width)
    w_time_t = jnp.transpose(w_time, (1, 2, 0)).reshape(3 * chan, width)
    w_group_t = jnp.transpose(w_group, (1, 2, 0)).reshape(3 * chan, width)
    w_gate_t = w_gate.T

    spread = [
        lax.all_to_all(pack(series_in, me, j, n_ser), SERIES_AXES, 0, 0, tiled=True)
        for j in range(2)
    ]
    group_w = around(w_group_t)
    gate_out_w = around(jnp.concatenate([w_gate_t, w_out], axis=0))
    gate_w, out_w = gate_out_w[:, :chan], gate_out_w[:, chan:]

    time_t = time_part(series_in, gain, w_time_t)
    time_rows = lax.all_to_all(time_t, "mp", 0, 0, tiled=True).reshape(
        members, ser // members, chan, patches
    )
    order = (me - jnp.array([0, 1, members - 1, 2], jnp.int32)) % members
    time_cols = project(jnp.take(time_rows, order, axis=0), out_w)
    time_cols = lax.all_to_all(time_cols, "mp", 0, 0, tiled=True).reshape(ser, chan, patches)

    group_col = group_of.reshape(-1, 1)
    group_row = group_of.reshape(1, -1)
    back = []
    for j in range(2):
        sent = group_part(spread[j], gain, group_w, gate_w, out_w, group_col, group_row)
        sent = sent.reshape(members * n_ser, 8, 2 * chan)
        sent = lax.all_to_all(sent, ("mp", *SERIES_AXES), 0, 0, tiled=True)
        back.append(sent.reshape(members * n_ser * 8, 2 * chan))
    out = join(time_cols, back[0], back[1])
    return jnp.transpose(out.reshape(ser, chan, patches), (0, 2, 1))


def solution(mesh):
    n_ser, n_mp = mesh.devices.shape
    split = Mesh(mesh.devices.reshape(n_ser // 2, 2, n_mp), ("sc", "core", "mp"))
    placed = (
        P(SERIES_AXES, None, None),
        P(),
        P(None, "mp", None),
        P(None, "mp", None),
        P(None, "mp"),
        P("mp", None),
        P(),
    )
    return jax.shard_map(
        per_device,
        mesh=split,
        in_specs=placed,
        out_specs=P(SERIES_AXES, None, "mp"),
        check_vma=False,
    )
```

```python
import jax
import jax.numpy as jnp
from jax import lax
from jax.experimental import pallas as pl
from jax.experimental.pallas import tpu as pltpu
from jax.sharding import Mesh
from jax.sharding import PartitionSpec as P

BF = jnp.bfloat16
F32 = jnp.float32
SERIES_AXES = ("sc", "core")
BIG = 2.0**50
DISTANCES = (0, 1, 3, 2)


def nt(a, b):
    return lax.dot_general(a, b, (((1,), (1,)), ((), ())), preferred_element_type=F32)


def nn(a, b):
    return lax.dot_general(a, b, (((1,), (0,)), ((), ())), preferred_element_type=F32)


def tn(a, b):
    return lax.dot_general(a, b, (((0,), (0,)), ((), ())), preferred_element_type=F32)


def cost(flops, moved, exps=0):
    return pl.CostEstimate(flops=flops, bytes_accessed=moved, transcendentals=exps)


def in_hbm(x):
    return pltpu.with_memory_space_constraint(x, pltpu.HBM)


def params(mib):
    return pltpu.CompilerParams(vmem_limit_bytes=mib << 20)


def normed_rows(x, gain):
    xf = x.astype(F32)
    mean_sq = jnp.mean(xf * xf, axis=-1, keepdims=True)
    return (xf * lax.rsqrt(mean_sq + 1e-06) * gain).astype(BF)


def half_kernel(core_ref, group_ref, gate_ref, out_ref, o_ref):
    at = 0
    for ref in (group_ref, gate_ref, out_ref):
        rows = ref.shape[0]
        o_ref[at : at + rows] = ref[...]
        at += rows


def half_weights(core, w_group_t, w_gate_t, w_out):
    weights = (w_group_t, w_gate_t, w_out)
    width = w_out.shape[1]
    rows = sum(w.shape[0] for w in weights) // 2
    return pl.pallas_call(
        half_kernel,
        out_shape=pltpu.HBM((rows, width), BF),
        grid_spec=pltpu.PrefetchScalarGridSpec(
            num_scalar_prefetch=1,
            grid=(1,),
            in_specs=[
                pl.BlockSpec((w.shape[0] // 2, width), lambda i, core: (core[0], 0))
                for w in weights
            ],
            out_specs=pl.BlockSpec((rows, width), lambda i, core: (0, 0)),
        ),
        compiler_params=params(16),
        cost_estimate=cost(0, 2 << 20),
        name="half",
    )(core, *map(in_hbm, weights))


def place(i):
    return (i // 2 % 2) * 8 + (i // 4) * 2 + i % 2


def pack_kernel(me_ref, x_ref, o_ref, tmp):
    ser, rows, _ = x_ref.shape
    blocks = tmp.shape[0]
    for i in range(ser):
        values = x_ref[i].astype(F32)
        for c in range(blocks):
            tmp[c, pl.ds(place(i), rows, stride=ser), :] = values[:, c * 128 : (c + 1) * 128]
    for c in range(blocks):
        o_ref[:, c * 128 : (c + 1) * 128] = tmp[c].astype(BF)


def pack(series_in, me, n_ser):
    ser, patches, width = series_in.shape
    n_mp = patches // (2 * n_ser)
    return pl.pallas_call(
        pack_kernel,
        out_shape=jax.ShapeDtypeStruct((n_ser * ser, 2 * width), BF),
        grid_spec=pltpu.PrefetchScalarGridSpec(
            num_scalar_prefetch=1,
            grid=(2,),
            in_specs=[pl.BlockSpec((ser, n_ser, width), lambda j, me: (0, j * n_mp + me[0], 0))],
            out_specs=pl.BlockSpec((n_ser * ser, width), lambda j, me: (0, j)),
            scratch_shapes=[pltpu.VMEM((width // 128, n_ser * ser, 128), F32)],
        ),
        compiler_params=params(16),
        cost_estimate=cost(0, 4 << 20),
        name="pack",
    )(me, in_hbm(series_in))


def time_kernel(me_ref, x_ref, gain_ref, w_ref, *refs):
    *outs_ref, w_q, w_k, w_v = refs
    results = []
    hd = 64
    heads = w_ref.shape[0] // (3 * hd)

    @pl.when(pl.program_id(0) == 0)
    def _():
        for h in range(heads):
            base = h * 3 * hd
            w_q[h * hd : (h + 1) * hd] = w_ref[base : base + hd]
            w_k[h * hd : (h + 1) * hd] = w_ref[base + hd : base + 2 * hd]
            w_v[h * hd : (h + 1) * hd] = w_ref[base + 2 * hd : base + 3 * hd]
        for w in (w_q, w_k, w_v):
            w[heads * hd :] = jnp.zeros((hd, w.shape[1]), BF)

    ser, rows, width = x_ref.shape
    normed = normed_rows(x_ref[...].reshape(ser * rows, width), gain_ref[...])
    queries = (nt(normed, w_q[...]) * 0.125).astype(BF)
    keys = nt(normed, w_k[...]).astype(BF)
    values = nt(normed, w_v[...]).astype(BF)
    lower = lax.broadcasted_iota(jnp.int32, (rows, 128), 1) < hd
    for i in range(ser):
        span = slice(i * rows, (i + 1) * rows)
        for b in range((heads + 1) // 2):
            at = slice(b * 128, (b + 1) * 128)
            q_b, k_b, v_b = queries[span, at], keys[span, at], values[span, at]
            outs = []
            for e in range(min(2, heads - 2 * b)):
                own = lower if e == 0 else ~lower
                k_e = jnp.where(own, k_b, jnp.zeros_like(k_b))
                v_e = jnp.where(own, v_b, jnp.ones_like(v_b))
                scores = nt(q_b, k_e)
                top = jnp.max(scores, axis=1, keepdims=True)
                outs.append(nn(jnp.exp(scores - top).astype(BF), v_e))
            if len(outs) == 2:
                num = jnp.where(lower, outs[0], outs[1])
                den = pltpu.roll(jnp.where(lower, outs[1], outs[0]), 64, 1)
            else:
                num, den = outs[0], pltpu.roll(outs[0], 64, 1)
            out = (num / den).T.astype(BF)
            results.append((i, b * 128, out if len(outs) == 2 else out[:hd]))
    per = pl.num_programs(0) // len(outs_ref)
    for k, o_ref in enumerate(outs_ref):

        def store():
            for i, first, out in results:
                o_ref[i, first : first + out.shape[0]] = out

        if len(outs_ref) == 1:
            store()
        else:
            pl.when(lax.div(pl.program_id(0), per) == k)(store)


def time_part(series_in, gain, w_time_t, me, distances, n_mp, step=2):
    ser, patches, width = series_in.shape
    chan = w_time_t.shape[0] // 3
    part = ser // n_mp
    steps = part // step

    def share(i, me):
        distance = distances[0]
        for k, other in enumerate(distances[1:]):
            distance = jnp.where(i >= (k + 1) * steps, other, distance)
        return (lax.rem(me[0] + distance, n_mp) * steps + lax.rem(i, steps), 0, 0)

    return pl.pallas_call(
        time_kernel,
        out_shape=(pltpu.HBM((part, chan, patches), BF),) * len(distances),
        grid_spec=pltpu.PrefetchScalarGridSpec(
            num_scalar_prefetch=1,
            grid=(len(distances) * steps,),
            in_specs=[
                pl.BlockSpec((step, patches, width), share),
                pl.BlockSpec((1, width), lambda i, me: (0, 0)),
                pl.BlockSpec((3 * chan, width), lambda i, me: (0, 0)),
            ],
            out_specs=[
                pl.BlockSpec(
                    (step, chan, patches),
                    lambda i, me, k=k: (jnp.clip(i - k * steps, 0, steps - 1), 0, 0),
                )
                for k in range(len(distances))
            ],
            scratch_shapes=[pltpu.VMEM((chan + 64, width), BF)] * 3,
        ),
        compiler_params=params(24),
        cost_estimate=cost(4 * 10**9 * len(distances), 4 << 20, 10**6),
        name="time",
    )(me, in_hbm(series_in), gain, in_hbm(w_time_t))


def gather_weights(core, group_ref, gate_ref, out_ref, pieces, w_q, w_k, w_v, w_gate, w_out, wg):
    hd = 64
    half_g, half_o = group_ref.shape[0] // 2, out_ref.shape[0] // 2
    chan = 2 * half_o
    w_gate[:chan] = gate_ref[...]
    w_out[:chan] = out_ref[...]
    wg[0] = group_ref[...]
    for k in range(2):
        which = core if k == 0 else 1 - core
        at_g = pl.multiple_of(which * half_g, 16)
        at_o = pl.multiple_of(which * half_o, 16)
        for r in (1, 2, 3):
            ref = pieces[4 * k + r - 1]
            first = ref.shape[0] if r == 3 else half_g
            wg[r, pl.ds(at_g, first), :] = ref[:first]
            skip = first
            if r == 3:
                ref = pieces[4 * k + 3]
                skip = half_g - first
                wg[r, pl.ds(at_g + first, skip), :] = ref[:skip]
            w_gate[pl.ds(r * chan + at_o, half_o), :] = ref[skip : skip + half_o]
            w_out[pl.ds(r * chan + at_o, half_o), :] = ref[skip + half_o : skip + 2 * half_o]
    heads_m = group_ref.shape[0] // (3 * hd)
    for h in range(4 * heads_m):
        m, base = h // heads_m, (h % heads_m) * 3 * hd
        w_q[h * hd : (h + 1) * hd] = wg[m, base : base + hd]
        w_k[h * hd : (h + 1) * hd] = wg[m, base + hd : base + 2 * hd]
        w_v[h * hd : (h + 1) * hd] = wg[m, base + 2 * hd : base + 3 * hd]


def project_kernel(me_ref, core_ref, t0_ref, t1_ref, t2_ref, t3_ref, w_ref, *refs):
    pieces, outs, w_t = refs[:6], refs[6:10], refs[10]
    ser, chan, patches = t0_ref.shape
    half = chan // 2

    @pl.when(pl.program_id(0) == 0)
    def _():
        blocks = [w_ref[...]]
        first = core_ref[0] == 0
        for mine, other in zip(pieces[:3], pieces[3:]):
            mine, other = mine[-half:], other[-half:]
            blocks += [jnp.where(first, mine, other), jnp.where(first, other, mine)]
        w_t[...] = jnp.concatenate(blocks, axis=0).T

    me = me_ref[0]
    for i in range(ser):
        rows = jnp.concatenate([t_ref[i] for t_ref in (t0_ref, t1_ref, t2_ref, t3_ref)], axis=0)
        for distance, o_ref in zip(DISTANCES, outs):
            at = pl.multiple_of(lax.rem(me + distance, 4) * chan, 16)
            o_ref[i] = nn(w_t[pl.ds(at, chan), :], rows).astype(BF)


def project(me, core, times, w_out, pieces):
    ser, chan, patches = times[0].shape
    width = w_out.shape[1]
    half = chan // 2
    spec = pl.BlockSpec((2, chan, patches), lambda i, me: (i, 0, 0))

    def last_rows(piece):
        rows = piece.shape[0]
        if rows % half:
            return pl.BlockSpec(piece.shape, lambda i, me: (0, 0))
        return pl.BlockSpec((half, width), lambda i, me: (rows // half - 1, 0))

    return pl.pallas_call(
        project_kernel,
        out_shape=(pltpu.HBM(times[0].shape, BF),) * 4,
        grid_spec=pltpu.PrefetchScalarGridSpec(
            num_scalar_prefetch=1,
            grid=(ser // 2,),
            in_specs=[pl.BlockSpec(memory_space=pltpu.SMEM)]
            + [spec] * 4
            + [pl.BlockSpec(w_out.shape, lambda i, me: (0, 0))]
            + [last_rows(p) for p in pieces],
            out_specs=[spec] * 4,
            scratch_shapes=[pltpu.VMEM((4 * chan, width), BF)],
        ),
        compiler_params=params(16),
        cost_estimate=cost(12 * 10**8, 4 << 20),
        name="project",
    )(me, core, *map(in_hbm, times), in_hbm(w_out), *map(in_hbm, pieces))


def group_kernel(core_ref, x_ref, gain_ref, gcol_ref, group_ref, gate_ref, out_ref, *refs):
    pieces = refs[:8]
    o_ref, wq_ref, wk_ref, wv_ref, wgate_ref, wout_ref, wg, kmat, qmat, vmat, gated = refs[8:]
    gather_weights(core_ref[0], group_ref, gate_ref, out_ref, pieces,
                   wq_ref, wk_ref, wv_ref, wgate_ref, wout_ref, wg)
    n = x_ref.shape[0]
    width = wq_ref.shape[1]
    blocks = kmat.shape[0]
    members = o_ref.shape[0]
    lanes = lax.broadcasted_iota(jnp.int32, (n, 128), 1)
    same = gcol_ref[...] == lanes
    k_mask = jnp.where(same, 0.0, -BIG).astype(BF)
    q_mask = jnp.where(same, BIG, 0.0).astype(BF)
    lower = lanes < 64
    for j in range(2):
        normed = normed_rows(x_ref[:, j * width : (j + 1) * width], gain_ref[...])
        queries = (nt(normed, wq_ref[...]) * 0.125).astype(BF)
        keys = nt(normed, wk_ref[...]).astype(BF)
        values = nt(normed, wv_ref[...]).astype(BF)
        for b in range(blocks):
            at = slice(b * 128, (b + 1) * 128)
            qmat[b] = queries[:, at]
            kmat[b] = keys[:, at]
            vmat[b] = values[:, at]

        for b in range(blocks):
            q_b = jnp.concatenate([qmat[b], q_mask], axis=1)
            k_b, v_b = kmat[b], vmat[b]
            outs = []
            for e in range(2):
                own = lower if e == 0 else ~lower
                k_e = jnp.concatenate([jnp.where(own, k_b, jnp.zeros_like(k_b)), k_mask], axis=1)
                v_e = jnp.where(own, v_b, jnp.ones_like(v_b))
                scores = nt(q_b, k_e)
                top = jnp.max(scores, axis=1, keepdims=True)
                outs.append(nn(jnp.exp(scores - top).astype(BF), v_e))
            num = jnp.where(lower, outs[0], outs[1])
            den = pltpu.roll(jnp.where(lower, outs[1], outs[0]), 64, 1)
            gated[b] = (num / den).astype(BF)

        gate = jax.nn.sigmoid(nt(normed, wgate_ref[...]))
        rows = jnp.concatenate(
            [
                (gate[:, b * 128 : (b + 1) * 128] * gated[b].astype(F32)).astype(BF)
                for b in range(blocks)
            ],
            axis=1,
        )
        out = nn(rows, wout_ref[...])
        cols = width // members
        for m in range(members):
            part = out[:, m * cols : (m + 1) * cols].reshape(n // 16, 16, cols)
            low, high = part[:, :8], part[:, 8:]
            o_ref[m, :, j * 8 : (j + 1) * 8] = jnp.concatenate(
                [low[:, :, :128], high[:, :, :128], low[:, :, 128:], high[:, :, 128:]], axis=-1
            ).astype(BF)


def group_part(core, rows, gain, group_col, w_group_t, w_gate_t, w_out, pieces, members):
    n = rows.shape[0]
    chan, width = w_out.shape
    full = (members * chan, width)
    vmem = pl.BlockSpec(memory_space=pltpu.VMEM)
    return pl.pallas_call(
        group_kernel,
        out_shape=pltpu.HBM((members, n // 16, 16, 2 * width // members), BF),
        in_specs=[pl.BlockSpec(memory_space=pltpu.SMEM)] + [vmem] * (6 + len(pieces)),
        out_specs=vmem,
        scratch_shapes=[pltpu.VMEM(full, BF)] * 5
        + [pltpu.VMEM((members, *w_group_t.shape), BF)]
        + [pltpu.VMEM((full[0] // 128, n, 128), BF)] * 4,
        compiler_params=params(44),
        cost_estimate=cost(14 * 10**9, 12 << 20, 7 * 10**6),
        name="group",
    )(
        core, in_hbm(rows), gain, group_col,
        *map(in_hbm, (w_group_t, w_gate_t, w_out, *pieces)),
    )


def join_kernel(me_ref, t0_ref, t1_ref, t2_ref, t3_ref, g_ref, o_ref, tmp):
    me = me_ref[0]
    for c in range(tmp.shape[0]):
        tmp[c] = g_ref[:, c * 128 : (c + 1) * 128].astype(F32)
    for distance, t_ref in zip(DISTANCES, (t0_ref, t1_ref, t2_ref, t3_ref)):
        m = lax.rem(me + 4 - distance, 4)
        for a in range(2):
            for j in range(2):
                rows = [
                    tmp[c, pl.ds(j * 8 + m * 2 + a, 128, stride=16), :].T
                    for c in range(tmp.shape[0])
                ]
                at = slice(j * 128, (j + 1) * 128)
                for e in range(2):
                    i = 2 * e + a
                    o_ref[m * 4 + i, :128, at] = (
                        t_ref[i, :128, at].astype(F32) + rows[e]
                    ).astype(BF)
                    o_ref[m * 4 + i, 128:, at] = (
                        t_ref[i, 128:, at].astype(F32) + rows[2][e * 64 : (e + 1) * 64]
                    ).astype(BF)


def join(me, pieces, group):
    part, cols, patches = pieces[0].shape
    vmem = pl.BlockSpec(memory_space=pltpu.VMEM)
    return pl.pallas_call(
        join_kernel,
        out_shape=jax.ShapeDtypeStruct((4 * part, cols, patches), BF),
        in_specs=[pl.BlockSpec(memory_space=pltpu.SMEM)] + [vmem] * 5,
        out_specs=vmem,
        scratch_shapes=[pltpu.VMEM((group.shape[1] // 128, group.shape[0], 128), F32)],
        compiler_params=params(20),
        cost_estimate=cost(0, 8 << 20),
        name="join",
    )(me, *pieces, group)


def after(value, *others):
    return lax.optimization_barrier((value, *others))[0]


def shift(value, by):
    n = lax.axis_size("mp")
    return lax.ppermute(value, "mp", [(i, (i + by) % n) for i in range(n)])


def swap(value):
    return lax.ppermute(value, "core", [(0, 1), (1, 0)])


def per_device(series_in, norm_gain, w_time, w_group, w_gate, w_out, group_of):
    ser, patches, width = series_in.shape
    members = lax.axis_size("mp")
    n_ser = lax.axis_size("sc") * lax.axis_size("core")
    chan = w_gate.shape[1]
    me = lax.axis_index("mp").reshape(1)
    core = lax.axis_index("core").reshape(1)
    gain = norm_gain.reshape(1, width)
    w_time_t = jnp.transpose(w_time, (1, 2, 0)).reshape(3 * chan, width)
    w_group_t = jnp.transpose(w_group, (1, 2, 0)).reshape(3 * chan, width)
    w_gate_t = w_gate.T

    half = half_weights(core, w_group_t, w_gate_t, w_out)
    below = shift(half, 1)
    above = shift(half, 3)
    packed = pack(after(series_in, half), me, n_ser)
    spread = lax.all_to_all(
        packed.reshape(n_ser, ser, 2 * width), SERIES_AXES, 0, 0, tiled=True
    ).reshape(n_ser * ser, 2 * width)

    sent_group = group_of.reshape(n_ser, members, 2, 2).transpose(0, 2, 1, 3).reshape(-1, 1)
    quarter = half.shape[0] // 2
    x = after(series_in, packed, sent_group)
    (two,) = time_part(x, gain, w_time_t, me, (2,), members)
    far_a = shift(after(below[:quarter], two), 1)
    far_b = shift(after(above[quarter:], two), 3)
    one, three = time_part(after(x, two), gain, w_time_t, me, (1, 3), members)
    near = [swap(after(below, one)), swap(after(above, one))]
    (own,) = time_part(after(x, one, far_a, far_b), gain, w_time_t, me, (0,), members)
    far = [swap(far_a), swap(far_b)]
    times = {0: own, 1: shift(one, 1), 3: shift(three, 3), 2: shift(two, 2)}
    cols = project(
        me, core, [after(times[d], own) for d in DISTANCES], w_out,
        [below, above, far_b, *near, far[1]],
    )
    pieces = [below, above, far_a, far_b, *near, *far]
    back = group_part(
        core, spread, gain, sent_group, after(w_group_t, *cols), w_gate_t, w_out, pieces, members
    )
    cols = [c if d == 0 else shift(c, d) for d, c in zip(DISTANCES, cols)]
    back, *cols = lax.optimization_barrier((back, *cols))
    back = back.reshape(members * n_ser, 16, 2 * chan)
    back = lax.all_to_all(back, ("mp", *SERIES_AXES), 0, 0, tiled=True)
    out = join(me, cols, back.reshape(members * n_ser * 16, 2 * chan))
    return jnp.transpose(out, (0, 2, 1))


def solution(mesh):
    n_ser, n_mp = mesh.devices.shape
    split = Mesh(mesh.devices.reshape(n_ser // 2, 2, n_mp), ("sc", "core", "mp"))
    placed = (
        P(SERIES_AXES, None, None),
        P(),
        P(None, "mp", None),
        P(None, "mp", None),
        P(None, "mp"),
        P("mp", None),
        P(),
    )
    return jax.shard_map(
        per_device,
        mesh=split,
        in_specs=placed,
        out_specs=P(SERIES_AXES, None, "mp"),
        check_vma=False,
    )
```

```python
import jax
import jax.numpy as jnp
from jax import lax
from jax.experimental import pallas as pl
from jax.experimental.pallas import tpu as pltpu
from jax.sharding import Mesh
from jax.sharding import PartitionSpec as P

BF = jnp.bfloat16
F32 = jnp.float32
SERIES_AXES = ("sc", "core")
BIG = 2.0**50
DISTANCES = (0, 1, 3, 2)


def nt(a, b):
    return lax.dot_general(a, b, (((1,), (1,)), ((), ())), preferred_element_type=F32)


def nn(a, b):
    return lax.dot_general(a, b, (((1,), (0,)), ((), ())), preferred_element_type=F32)


def tn(a, b):
    return lax.dot_general(a, b, (((0,), (0,)), ((), ())), preferred_element_type=F32)


def cost(flops, moved, exps=0):
    return pl.CostEstimate(flops=flops, bytes_accessed=moved, transcendentals=exps)


def in_hbm(x):
    return pltpu.with_memory_space_constraint(x, pltpu.HBM)


def params(mib):
    return pltpu.CompilerParams(vmem_limit_bytes=mib << 20)


def normed_rows(x, gain):
    xf = x.astype(F32)
    mean_sq = jnp.mean(xf * xf, axis=-1, keepdims=True)
    return (xf * lax.rsqrt(mean_sq + 1e-06) * gain).astype(BF)


def half_kernel(core_ref, group_ref, gate_ref, out_ref, o_ref):
    at = 0
    for ref in (group_ref, gate_ref, out_ref):
        rows = ref.shape[0]
        o_ref[at : at + rows] = ref[...]
        at += rows


def half_weights(core, w_group_t, w_gate_t, w_out):
    weights = (w_group_t, w_gate_t, w_out)
    width = w_out.shape[1]
    rows = sum(w.shape[0] for w in weights) // 2
    return pl.pallas_call(
        half_kernel,
        out_shape=pltpu.HBM((rows, width), BF),
        grid_spec=pltpu.PrefetchScalarGridSpec(
            num_scalar_prefetch=1,
            grid=(1,),
            in_specs=[
                pl.BlockSpec((w.shape[0] // 2, width), lambda i, core: (core[0], 0))
                for w in weights
            ],
            out_specs=pl.BlockSpec((rows, width), lambda i, core: (0, 0)),
        ),
        compiler_params=params(16),
        cost_estimate=cost(0, 2 << 20),
        name="half",
    )(core, *map(in_hbm, weights))


def place(i):
    return (i // 2 % 2) * 8 + (i // 4) * 2 + i % 2


def pack_kernel(me_ref, x_ref, o_ref, tmp):
    ser, rows, _ = x_ref.shape
    blocks = tmp.shape[0]
    for i in range(ser):
        values = x_ref[i].astype(F32)
        for c in range(blocks):
            tmp[c, pl.ds(place(i), rows, stride=ser), :] = values[:, c * 128 : (c + 1) * 128]
    for c in range(blocks):
        o_ref[:, c * 128 : (c + 1) * 128] = tmp[c].astype(BF)


def pack(series_in, me, n_ser):
    ser, patches, width = series_in.shape
    n_mp = patches // (2 * n_ser)
    return pl.pallas_call(
        pack_kernel,
        out_shape=jax.ShapeDtypeStruct((n_ser * ser, 2 * width), BF),
        grid_spec=pltpu.PrefetchScalarGridSpec(
            num_scalar_prefetch=1,
            grid=(2,),
            in_specs=[pl.BlockSpec((ser, n_ser, width), lambda j, me: (0, j * n_mp + me[0], 0))],
            out_specs=pl.BlockSpec((n_ser * ser, width), lambda j, me: (0, j)),
            scratch_shapes=[pltpu.VMEM((width // 128, n_ser * ser, 128), F32)],
        ),
        compiler_params=params(16),
        cost_estimate=cost(0, 4 << 20),
        name="pack",
    )(me, in_hbm(series_in))


def time_kernel(x_ref, gain_ref, w_ref, buf_ref, o_ref, w_q, w_k, w_v):
    hd = 64
    heads = w_ref.shape[0] // (3 * hd)

    @pl.when(pl.program_id(0) == 0)
    def _():
        for h in range(heads):
            base = h * 3 * hd
            w_q[h * hd : (h + 1) * hd] = w_ref[base : base + hd]
            w_k[h * hd : (h + 1) * hd] = w_ref[base + hd : base + 2 * hd]
            w_v[h * hd : (h + 1) * hd] = w_ref[base + 2 * hd : base + 3 * hd]
        for w in (w_q, w_k, w_v):
            w[heads * hd :] = jnp.zeros((hd, w.shape[1]), BF)

    ser, rows, width = x_ref.shape
    normed = normed_rows(x_ref[...].reshape(ser * rows, width), gain_ref[...])
    queries = (nt(normed, w_q[...]) * 0.125).astype(BF)
    keys = nt(normed, w_k[...]).astype(BF)
    values = nt(normed, w_v[...]).astype(BF)
    lower = lax.broadcasted_iota(jnp.int32, (rows, 128), 1) < hd
    for i in range(ser):
        span = slice(i * rows, (i + 1) * rows)
        for b in range((heads + 1) // 2):
            at = slice(b * 128, (b + 1) * 128)
            q_b, k_b, v_b = queries[span, at], keys[span, at], values[span, at]
            outs = []
            for e in range(min(2, heads - 2 * b)):
                own = lower if e == 0 else ~lower
                k_e = jnp.where(own, k_b, jnp.zeros_like(k_b))
                v_e = jnp.where(own, v_b, jnp.ones_like(v_b))
                scores = nt(q_b, k_e)
                top = jnp.max(scores, axis=1, keepdims=True)
                outs.append(nn(jnp.exp(scores - top).astype(BF), v_e))
            if len(outs) == 2:
                num = jnp.where(lower, outs[0], outs[1])
                den = pltpu.roll(jnp.where(lower, outs[1], outs[0]), 64, 1)
            else:
                num, den = outs[0], pltpu.roll(outs[0], 64, 1)
            out = (num / den).T.astype(BF)
            if len(outs) == 2:
                o_ref[i, at] = out
            else:
                o_ref[i, b * 128 : b * 128 + hd] = out[:hd]


def time_part(series_in, gain, w_time_t, buffer, first, last, step=2):
    ser, patches, width = series_in.shape
    chan = w_time_t.shape[0] // 3
    out = pltpu.HBM((ser, chan, patches), BF)
    base = first // step
    args = (in_hbm(series_in), gain, in_hbm(w_time_t)) + (() if buffer is None else (in_hbm(buffer),))

    def kernel(x_ref, gain_ref, w_ref, *refs):
        time_kernel(x_ref, gain_ref, w_ref, None, *refs[len(args) - 3 :])

    return pl.pallas_call(
        kernel,
        out_shape=out,
        grid=((last - first) // step,),
        in_specs=[
            pl.BlockSpec((step, patches, width), lambda i: (base + i, 0, 0)),
            pl.BlockSpec((1, width), lambda i: (0, 0)),
            pl.BlockSpec((3 * chan, width), lambda i: (0, 0)),
        ]
        + [pl.BlockSpec(memory_space=pl.ANY)] * (len(args) - 3),
        out_specs=pl.BlockSpec((step, chan, patches), lambda i: (base + i, 0, 0)),
        scratch_shapes=[pltpu.VMEM((chan + 64, width), BF)] * 3,
        input_output_aliases={} if buffer is None else {3: 0},
        compiler_params=params(20),
        cost_estimate=cost(10**8, 1 << 18),
        name="time",
    )(*args)


def gather_weights(core, group_ref, gate_ref, out_ref, pieces, w_q, w_k, w_v, w_gate, w_out, wg):
    hd = 64
    half_g, half_o = group_ref.shape[0] // 2, out_ref.shape[0] // 2
    chan = 2 * half_o
    w_gate[:chan] = gate_ref[...]
    w_out[:chan] = out_ref[...]
    wg[0] = group_ref[...]
    for k in range(2):
        which = core if k == 0 else 1 - core
        at_g = pl.multiple_of(which * half_g, 16)
        at_o = pl.multiple_of(which * half_o, 16)
        for r in (1, 2, 3):
            ref = pieces[4 * k + r - 1]
            first = ref.shape[0] if r == 3 else half_g
            wg[r, pl.ds(at_g, first), :] = ref[:first]
            skip = first
            if r == 3:
                ref = pieces[4 * k + 3]
                skip = half_g - first
                wg[r, pl.ds(at_g + first, skip), :] = ref[:skip]
            w_gate[pl.ds(r * chan + at_o, half_o), :] = ref[skip : skip + half_o]
            w_out[pl.ds(r * chan + at_o, half_o), :] = ref[skip + half_o : skip + 2 * half_o]
    heads_m = group_ref.shape[0] // (3 * hd)
    for h in range(4 * heads_m):
        m, base = h // heads_m, (h % heads_m) * 3 * hd
        w_q[h * hd : (h + 1) * hd] = wg[m, base : base + hd]
        w_k[h * hd : (h + 1) * hd] = wg[m, base + hd : base + 2 * hd]
        w_v[h * hd : (h + 1) * hd] = wg[m, base + 2 * hd : base + 3 * hd]


def project_kernel(me_ref, t_ref, w_ref, *refs):
    outs, w_t = refs[:4], refs[4]
    members, ser, chan, patches = t_ref.shape

    @pl.when(pl.program_id(0) == 0)
    def _():
        w_t[...] = w_ref[...].T

    me = me_ref[0]
    for i in range(ser):
        rows = jnp.concatenate(
            [t_ref[lax.rem(me + 4 - distance, 4), i] for distance in DISTANCES], axis=0
        )
        for distance, o_ref in zip(DISTANCES, outs):
            at = pl.multiple_of(lax.rem(me + distance, 4) * chan, 16)
            o_ref[i] = nn(w_t[pl.ds(at, chan), :], rows).astype(BF)


def project(me, pieces, w_out):
    members, ser, chan, patches = pieces.shape
    spec = pl.BlockSpec((2, chan, patches), lambda i, me: (i, 0, 0))
    return pl.pallas_call(
        project_kernel,
        out_shape=(jax.ShapeDtypeStruct(pieces.shape[1:], BF),) * 4,
        grid_spec=pltpu.PrefetchScalarGridSpec(
            num_scalar_prefetch=1,
            grid=(ser // 2,),
            in_specs=[
                pl.BlockSpec((members, 2, chan, patches), lambda i, me: (0, i, 0, 0)),
                pl.BlockSpec(w_out.shape, lambda i, me: (0, 0)),
            ],
            out_specs=[spec] * 4,
            scratch_shapes=[pltpu.VMEM(w_out.shape, BF)],
        ),
        compiler_params=params(16),
        cost_estimate=cost(12 * 10**8, 4 << 20),
        name="project",
    )(me, pieces, w_out)


def group_kernel(core_ref, x_ref, gain_ref, gcol_ref, group_ref, gate_ref, out_ref, *refs):
    pieces = refs[:8]
    o_ref, wout_ref, wq_ref, wk_ref, wv_ref, wgate_ref, wg, kmat, qmat, vmat, gated = refs[8:]
    gather_weights(core_ref[0], group_ref, gate_ref, out_ref, pieces,
                   wq_ref, wk_ref, wv_ref, wgate_ref, wout_ref, wg)
    n = x_ref.shape[0]
    width = wq_ref.shape[1]
    blocks = kmat.shape[0]
    members = o_ref.shape[0]
    lanes = lax.broadcasted_iota(jnp.int32, (n, 128), 1)
    same = gcol_ref[...] == lanes
    k_mask = jnp.where(same, 0.0, -BIG).astype(BF)
    q_mask = jnp.where(same, BIG, 0.0).astype(BF)
    lower = lanes < 64
    for j in range(2):
        normed = normed_rows(x_ref[:, j * width : (j + 1) * width], gain_ref[...])
        queries = (nt(normed, wq_ref[...]) * 0.125).astype(BF)
        keys = nt(normed, wk_ref[...]).astype(BF)
        values = nt(normed, wv_ref[...]).astype(BF)
        for b in range(blocks):
            at = slice(b * 128, (b + 1) * 128)
            qmat[b] = queries[:, at]
            kmat[b] = keys[:, at]
            vmat[b] = values[:, at]

        for b in range(blocks):
            q_b = jnp.concatenate([qmat[b], q_mask], axis=1)
            k_b, v_b = kmat[b], vmat[b]
            outs = []
            for e in range(2):
                own = lower if e == 0 else ~lower
                k_e = jnp.concatenate([jnp.where(own, k_b, jnp.zeros_like(k_b)), k_mask], axis=1)
                v_e = jnp.where(own, v_b, jnp.ones_like(v_b))
                scores = nt(q_b, k_e)
                top = jnp.max(scores, axis=1, keepdims=True)
                outs.append(nn(jnp.exp(scores - top).astype(BF), v_e))
            num = jnp.where(lower, outs[0], outs[1])
            den = pltpu.roll(jnp.where(lower, outs[1], outs[0]), 64, 1)
            gated[b] = (num / den).astype(BF)

        gate = jax.nn.sigmoid(nt(normed, wgate_ref[...]))
        rows = jnp.concatenate(
            [
                (gate[:, b * 128 : (b + 1) * 128] * gated[b].astype(F32)).astype(BF)
                for b in range(blocks)
            ],
            axis=1,
        )
        out = nn(rows, wout_ref[...])
        cols = width // members
        for m in range(members):
            part = out[:, m * cols : (m + 1) * cols].reshape(n // 16, 16, cols)
            low, high = part[:, :8], part[:, 8:]
            o_ref[m, :, j * 8 : (j + 1) * 8] = jnp.concatenate(
                [low[:, :, :128], high[:, :, :128], low[:, :, 128:], high[:, :, 128:]], axis=-1
            ).astype(BF)


def group_part(core, rows, gain, group_col, w_group_t, w_gate_t, w_out, pieces, members):
    n = rows.shape[0]
    chan, width = w_out.shape
    full = (members * chan, width)
    vmem = pl.BlockSpec(memory_space=pltpu.VMEM)
    return pl.pallas_call(
        group_kernel,
        out_shape=(
            pltpu.HBM((members, n // 16, 16, 2 * width // members), BF),
            jax.ShapeDtypeStruct(full, BF),
        ),
        in_specs=[pl.BlockSpec(memory_space=pltpu.SMEM)] + [vmem] * (6 + len(pieces)),
        out_specs=(vmem, vmem),
        scratch_shapes=[pltpu.VMEM(full, BF)] * 4
        + [pltpu.VMEM((members, *w_group_t.shape), BF)]
        + [pltpu.VMEM((full[0] // 128, n, 128), BF)] * 4,
        compiler_params=params(44),
        cost_estimate=cost(14 * 10**9, 12 << 20, 7 * 10**6),
        name="group",
    )(
        core, in_hbm(rows), gain, group_col,
        *map(in_hbm, (w_group_t, w_gate_t, w_out, *pieces)),
    )


def join_kernel(me_ref, t0_ref, t1_ref, t2_ref, t3_ref, g_ref, o_ref, tmp):
    me = me_ref[0]
    for c in range(tmp.shape[0]):
        tmp[c] = g_ref[:, c * 128 : (c + 1) * 128].astype(F32)
    for distance, t_ref in zip(DISTANCES, (t0_ref, t1_ref, t2_ref, t3_ref)):
        m = lax.rem(me + 4 - distance, 4)
        for a in range(2):
            for j in range(2):
                rows = [
                    tmp[c, pl.ds(j * 8 + m * 2 + a, 128, stride=16), :].T
                    for c in range(tmp.shape[0])
                ]
                at = slice(j * 128, (j + 1) * 128)
                for e in range(2):
                    i = 2 * e + a
                    o_ref[m * 4 + i, :128, at] = (
                        t_ref[i, :128, at].astype(F32) + rows[e]
                    ).astype(BF)
                    o_ref[m * 4 + i, 128:, at] = (
                        t_ref[i, 128:, at].astype(F32) + rows[2][e * 64 : (e + 1) * 64]
                    ).astype(BF)


def join(me, pieces, group):
    part, cols, patches = pieces[0].shape
    vmem = pl.BlockSpec(memory_space=pltpu.VMEM)
    return pl.pallas_call(
        join_kernel,
        out_shape=jax.ShapeDtypeStruct((4 * part, cols, patches), BF),
        in_specs=[pl.BlockSpec(memory_space=pltpu.SMEM)] + [vmem] * 5,
        out_specs=vmem,
        scratch_shapes=[pltpu.VMEM((group.shape[1] // 128, group.shape[0], 128), F32)],
        compiler_params=params(20),
        cost_estimate=cost(0, 8 << 20),
        name="join",
    )(me, *pieces, group)


def after(value, *others):
    return lax.optimization_barrier((value, *others))[0]


def shift(value, by):
    n = lax.axis_size("mp")
    return lax.ppermute(value, "mp", [(i, (i + by) % n) for i in range(n)])


def swap(value):
    return lax.ppermute(value, "core", [(0, 1), (1, 0)])


def per_device(series_in, norm_gain, w_time, w_group, w_gate, w_out, group_of):
    ser, patches, width = series_in.shape
    members = lax.axis_size("mp")
    n_ser = lax.axis_size("sc") * lax.axis_size("core")
    chan = w_gate.shape[1]
    me = lax.axis_index("mp").reshape(1)
    core = lax.axis_index("core").reshape(1)
    gain = norm_gain.reshape(1, width)
    w_time_t = jnp.transpose(w_time, (1, 2, 0)).reshape(3 * chan, width)
    w_group_t = jnp.transpose(w_group, (1, 2, 0)).reshape(3 * chan, width)
    w_gate_t = w_gate.T

    half = half_weights(core, w_group_t, w_gate_t, w_out)
    below = shift(half, 1)
    above = shift(half, 3)
    packed = pack(after(series_in, half), me, n_ser)
    spread = lax.all_to_all(
        packed.reshape(n_ser, ser, 2 * width), SERIES_AXES, 0, 0, tiled=True
    ).reshape(n_ser * ser, 2 * width)

    sent_group = group_of.reshape(n_ser, members, 2, 2).transpose(0, 2, 1, 3).reshape(-1, 1)
    quarter = half.shape[0] // 2
    x = after(series_in, packed, sent_group)
    part = ser // 2
    times = time_part(x, gain, w_time_t, None, 0, part)
    far_a = shift(after(below[:quarter], times), 1)
    far_b = shift(after(above[quarter:], times), 3)
    near = [swap(after(below, times)), swap(after(above, times))]
    times = time_part(x, gain, w_time_t, after(times, *near), part, ser)
    far = [swap(after(far_a, times)), swap(after(far_b, times))]
    pieces = [below, above, far_a, far_b, *near, *far]
    back, out_w = group_part(
        core, spread, gain, sent_group, after(w_group_t, times), w_gate_t, w_out, pieces, members
    )
    times = lax.all_to_all(times, "mp", 0, 0, tiled=True)
    back, times = lax.optimization_barrier((back, times))
    back = back.reshape(members * n_ser, 16, 2 * chan)
    back = lax.all_to_all(back, ("mp", *SERIES_AXES), 0, 0, tiled=True)

    cols = project(me, times.reshape(members, ser // members, chan, patches), out_w)
    cols = [c if d == 0 else shift(c, d) for d, c in zip(DISTANCES, cols)]
    out = join(me, cols, back.reshape(members * n_ser * 16, 2 * chan))
    return jnp.transpose(out, (0, 2, 1))


def solution(mesh):
    n_ser, n_mp = mesh.devices.shape
    split = Mesh(mesh.devices.reshape(n_ser // 2, 2, n_mp), ("sc", "core", "mp"))
    placed = (
        P(SERIES_AXES, None, None),
        P(),
        P(None, "mp", None),
        P(None, "mp", None),
        P(None, "mp"),
        P("mp", None),
        P(),
    )
    return jax.shard_map(
        per_device,
        mesh=split,
        in_specs=placed,
        out_specs=P(SERIES_AXES, None, "mp"),
        check_vma=False,
    )
```

```python
import jax
import jax.numpy as jnp
from jax import lax
from jax.experimental import pallas as pl
from jax.experimental.pallas import tpu as pltpu
from jax.sharding import Mesh
from jax.sharding import PartitionSpec as P

BF = jnp.bfloat16
F32 = jnp.float32
SERIES_AXES = ("sc", "core")
BIG = 2.0**50
DISTANCES = (0, 1, 3, 2)


def nt(a, b):
    return lax.dot_general(a, b, (((1,), (1,)), ((), ())), preferred_element_type=F32)


def nn(a, b):
    return lax.dot_general(a, b, (((1,), (0,)), ((), ())), preferred_element_type=F32)


def tn(a, b):
    return lax.dot_general(a, b, (((0,), (0,)), ((), ())), preferred_element_type=F32)


def cost(flops, moved, exps=0):
    return pl.CostEstimate(flops=flops, bytes_accessed=moved, transcendentals=exps)


def in_hbm(x):
    return pltpu.with_memory_space_constraint(x, pltpu.HBM)


def params(mib):
    return pltpu.CompilerParams(vmem_limit_bytes=mib << 20)


def normed_rows(x, gain):
    xf = x.astype(F32)
    mean_sq = jnp.mean(xf * xf, axis=-1, keepdims=True)
    return (xf * lax.rsqrt(mean_sq + 1e-06) * gain).astype(BF)


def half_kernel(core_ref, group_ref, gate_ref, out_ref, o_ref):
    at = 0
    for ref in (group_ref, gate_ref, out_ref):
        rows = ref.shape[0]
        o_ref[at : at + rows] = ref[...]
        at += rows


def half_weights(core, w_group_t, w_gate_t, w_out):
    weights = (w_group_t, w_gate_t, w_out)
    width = w_out.shape[1]
    rows = sum(w.shape[0] for w in weights) // 2
    return pl.pallas_call(
        half_kernel,
        out_shape=pltpu.HBM((rows, width), BF),
        grid_spec=pltpu.PrefetchScalarGridSpec(
            num_scalar_prefetch=1,
            grid=(1,),
            in_specs=[
                pl.BlockSpec((w.shape[0] // 2, width), lambda i, core: (core[0], 0))
                for w in weights
            ],
            out_specs=pl.BlockSpec((rows, width), lambda i, core: (0, 0)),
        ),
        compiler_params=params(16),
        cost_estimate=cost(0, 2 << 20),
        name="half",
    )(core, *map(in_hbm, weights))


def place(i):
    return (i // 2 % 2) * 8 + (i // 4) * 2 + i % 2


def pack_kernel(me_ref, x_ref, o_ref, tmp):
    ser, rows, _ = x_ref.shape
    blocks = tmp.shape[0]
    for i in range(ser):
        values = x_ref[i].astype(F32)
        for c in range(blocks):
            tmp[c, pl.ds(place(i), rows, stride=ser), :] = values[:, c * 128 : (c + 1) * 128]
    for c in range(blocks):
        o_ref[:, c * 128 : (c + 1) * 128] = tmp[c].astype(BF)


def pack(series_in, me, n_ser):
    ser, patches, width = series_in.shape
    n_mp = patches // (2 * n_ser)
    return pl.pallas_call(
        pack_kernel,
        out_shape=jax.ShapeDtypeStruct((n_ser * ser, 2 * width), BF),
        grid_spec=pltpu.PrefetchScalarGridSpec(
            num_scalar_prefetch=1,
            grid=(2,),
            in_specs=[pl.BlockSpec((ser, n_ser, width), lambda j, me: (0, j * n_mp + me[0], 0))],
            out_specs=pl.BlockSpec((n_ser * ser, width), lambda j, me: (0, j)),
            scratch_shapes=[pltpu.VMEM((width // 128, n_ser * ser, 128), F32)],
        ),
        compiler_params=params(16),
        cost_estimate=cost(0, 4 << 20),
        name="pack",
    )(me, in_hbm(series_in))


def time_kernel(x_ref, gain_ref, w_ref, buf_ref, o_ref, w_q, w_k, w_v):
    hd = 64
    heads = w_ref.shape[0] // (3 * hd)

    @pl.when(pl.program_id(0) == 0)
    def _():
        for h in range(heads):
            base = h * 3 * hd
            w_q[h * hd : (h + 1) * hd] = w_ref[base : base + hd]
            w_k[h * hd : (h + 1) * hd] = w_ref[base + hd : base + 2 * hd]
            w_v[h * hd : (h + 1) * hd] = w_ref[base + 2 * hd : base + 3 * hd]
        for w in (w_q, w_k, w_v):
            w[heads * hd :] = jnp.zeros((hd, w.shape[1]), BF)

    ser, rows, width = x_ref.shape
    normed = normed_rows(x_ref[...].reshape(ser * rows, width), gain_ref[...])
    queries = (nt(normed, w_q[...]) * 0.125).astype(BF)
    keys = nt(normed, w_k[...]).astype(BF)
    values = nt(normed, w_v[...]).astype(BF)
    lower = lax.broadcasted_iota(jnp.int32, (rows, 128), 1) < hd
    for i in range(ser):
        span = slice(i * rows, (i + 1) * rows)
        for b in range((heads + 1) // 2):
            at = slice(b * 128, (b + 1) * 128)
            q_b, k_b, v_b = queries[span, at], keys[span, at], values[span, at]
            outs = []
            for e in range(min(2, heads - 2 * b)):
                own = lower if e == 0 else ~lower
                k_e = jnp.where(own, k_b, jnp.zeros_like(k_b))
                v_e = jnp.where(own, v_b, jnp.ones_like(v_b))
                scores = nt(q_b, k_e)
                top = jnp.max(scores, axis=1, keepdims=True)
                outs.append(nn(jnp.exp(scores - top).astype(BF), v_e))
            if len(outs) == 2:
                num = jnp.where(lower, outs[0], outs[1])
                den = pltpu.roll(jnp.where(lower, outs[1], outs[0]), 64, 1)
            else:
                num, den = outs[0], pltpu.roll(outs[0], 64, 1)
            out = (num / den).T.astype(BF)
            if len(outs) == 2:
                o_ref[i, at] = out
            else:
                o_ref[i, b * 128 : b * 128 + hd] = out[:hd]


def time_part(series_in, gain, w_time_t, buffer, first, last, step=2):
    ser, patches, width = series_in.shape
    chan = w_time_t.shape[0] // 3
    out = pltpu.HBM((ser, chan, patches), BF)
    base = first // step
    args = (in_hbm(series_in), gain, in_hbm(w_time_t)) + (() if buffer is None else (in_hbm(buffer),))

    def kernel(x_ref, gain_ref, w_ref, *refs):
        time_kernel(x_ref, gain_ref, w_ref, None, *refs[len(args) - 3 :])

    return pl.pallas_call(
        kernel,
        out_shape=out,
        grid=((last - first) // step,),
        in_specs=[
            pl.BlockSpec((step, patches, width), lambda i: (base + i, 0, 0)),
            pl.BlockSpec((1, width), lambda i: (0, 0)),
            pl.BlockSpec((3 * chan, width), lambda i: (0, 0)),
        ]
        + [pl.BlockSpec(memory_space=pl.ANY)] * (len(args) - 3),
        out_specs=pl.BlockSpec((step, chan, patches), lambda i: (base + i, 0, 0)),
        scratch_shapes=[pltpu.VMEM((chan + 64, width), BF)] * 3,
        input_output_aliases={} if buffer is None else {3: 0},
        compiler_params=params(20),
        cost_estimate=cost(10**8, 1 << 18),
        name="time",
    )(*args)


def gather_weights(core, group_ref, gate_ref, out_ref, pieces, w_q, w_k, w_v, w_gate, w_out, wg):
    hd = 64
    half_g, half_o = group_ref.shape[0] // 2, out_ref.shape[0] // 2
    chan = 2 * half_o
    w_gate[:chan] = gate_ref[...]
    w_out[:chan] = out_ref[...]
    wg[0] = group_ref[...]
    for k in range(2):
        which = core if k == 0 else 1 - core
        at_g = pl.multiple_of(which * half_g, 16)
        at_o = pl.multiple_of(which * half_o, 16)
        for r in (1, 2, 3):
            ref = pieces[4 * k + r - 1]
            first = ref.shape[0] if r == 3 else half_g
            wg[r, pl.ds(at_g, first), :] = ref[:first]
            skip = first
            if r == 3:
                ref = pieces[4 * k + 3]
                skip = half_g - first
                wg[r, pl.ds(at_g + first, skip), :] = ref[:skip]
            w_gate[pl.ds(r * chan + at_o, half_o), :] = ref[skip : skip + half_o]
            w_out[pl.ds(r * chan + at_o, half_o), :] = ref[skip + half_o : skip + 2 * half_o]
    heads_m = group_ref.shape[0] // (3 * hd)
    for h in range(4 * heads_m):
        m, base = h // heads_m, (h % heads_m) * 3 * hd
        w_q[h * hd : (h + 1) * hd] = wg[m, base : base + hd]
        w_k[h * hd : (h + 1) * hd] = wg[m, base + hd : base + 2 * hd]
        w_v[h * hd : (h + 1) * hd] = wg[m, base + 2 * hd : base + 3 * hd]


def project_kernel(me_ref, t_ref, w_ref, *refs):
    outs, w_t = refs[:4], refs[4]
    members, ser, chan, patches = t_ref.shape

    @pl.when(pl.program_id(0) == 0)
    def _():
        w_t[...] = w_ref[...].T

    me = me_ref[0]
    for i in range(ser):
        rows = jnp.concatenate(
            [t_ref[lax.rem(me + 4 - distance, 4), i] for distance in DISTANCES], axis=0
        )
        for distance, o_ref in zip(DISTANCES, outs):
            at = pl.multiple_of(lax.rem(me + distance, 4) * chan, 16)
            o_ref[i] = nn(w_t[pl.ds(at, chan), :], rows).astype(BF)


def project(me, pieces, w_out):
    members, ser, chan, patches = pieces.shape
    spec = pl.BlockSpec((2, chan, patches), lambda i, me: (i, 0, 0))
    return pl.pallas_call(
        project_kernel,
        out_shape=(jax.ShapeDtypeStruct(pieces.shape[1:], BF),) * 4,
        grid_spec=pltpu.PrefetchScalarGridSpec(
            num_scalar_prefetch=1,
            grid=(ser // 2,),
            in_specs=[
                pl.BlockSpec((members, 2, chan, patches), lambda i, me: (0, i, 0, 0)),
                pl.BlockSpec(w_out.shape, lambda i, me: (0, 0)),
            ],
            out_specs=[spec] * 4,
            scratch_shapes=[pltpu.VMEM(w_out.shape, BF)],
        ),
        compiler_params=params(16),
        cost_estimate=cost(12 * 10**8, 4 << 20),
        name="project",
    )(me, pieces, in_hbm(w_out))


def group_kernel(core_ref, x_ref, gain_ref, gcol_ref, group_ref, gate_ref, out_ref, *refs):
    pieces = refs[:8]
    o_ref, wout_ref, wq_ref, wk_ref, wv_ref, wgate_ref, wg, kmat, qmat, vmat, gated = refs[8:]
    gather_weights(core_ref[0], group_ref, gate_ref, out_ref, pieces,
                   wq_ref, wk_ref, wv_ref, wgate_ref, wout_ref, wg)
    n = x_ref.shape[0]
    width = wq_ref.shape[1]
    blocks = kmat.shape[0]
    members = o_ref.shape[0]
    lanes = lax.broadcasted_iota(jnp.int32, (n, 128), 1)
    same = gcol_ref[...] == lanes
    k_mask = jnp.where(same, 0.0, -BIG).astype(BF)
    q_mask = jnp.where(same, BIG, 0.0).astype(BF)
    lower = lanes < 64
    for j in range(2):
        normed = normed_rows(x_ref[:, j * width : (j + 1) * width], gain_ref[...])
        queries = (nt(normed, wq_ref[...]) * 0.125).astype(BF)
        keys = nt(normed, wk_ref[...]).astype(BF)
        values = nt(normed, wv_ref[...]).astype(BF)
        for b in range(blocks):
            at = slice(b * 128, (b + 1) * 128)
            qmat[b] = queries[:, at]
            kmat[b] = keys[:, at]
            vmat[b] = values[:, at]

        for b in range(blocks):
            q_b = jnp.concatenate([qmat[b], q_mask], axis=1)
            k_b, v_b = kmat[b], vmat[b]
            outs = []
            for e in range(2):
                own = lower if e == 0 else ~lower
                k_e = jnp.concatenate([jnp.where(own, k_b, jnp.zeros_like(k_b)), k_mask], axis=1)
                v_e = jnp.where(own, v_b, jnp.ones_like(v_b))
                scores = nt(q_b, k_e)
                top = jnp.max(scores, axis=1, keepdims=True)
                outs.append(nn(jnp.exp(scores - top).astype(BF), v_e))
            num = jnp.where(lower, outs[0], outs[1])
            den = pltpu.roll(jnp.where(lower, outs[1], outs[0]), 64, 1)
            gated[b] = (num / den).astype(BF)

        gate = jax.nn.sigmoid(nt(normed, wgate_ref[...]))
        rows = jnp.concatenate(
            [
                (gate[:, b * 128 : (b + 1) * 128] * gated[b].astype(F32)).astype(BF)
                for b in range(blocks)
            ],
            axis=1,
        )
        out = nn(rows, wout_ref[...])
        cols = width // members
        for m in range(members):
            part = out[:, m * cols : (m + 1) * cols].reshape(n // 16, 16, cols)
            low, high = part[:, :8], part[:, 8:]
            o_ref[m, :, j * 8 : (j + 1) * 8] = jnp.concatenate(
                [low[:, :, :128], high[:, :, :128], low[:, :, 128:], high[:, :, 128:]], axis=-1
            ).astype(BF)


def group_part(core, rows, gain, group_col, w_group_t, w_gate_t, w_out, pieces, members):
    n = rows.shape[0]
    chan, width = w_out.shape
    full = (members * chan, width)
    vmem = pl.BlockSpec(memory_space=pltpu.VMEM)
    return pl.pallas_call(
        group_kernel,
        out_shape=(
            pltpu.HBM((members, n // 16, 16, 2 * width // members), BF),
            pltpu.HBM(full, BF),
        ),
        in_specs=[pl.BlockSpec(memory_space=pltpu.SMEM)] + [vmem] * (6 + len(pieces)),
        out_specs=(vmem, vmem),
        scratch_shapes=[pltpu.VMEM(full, BF)] * 4
        + [pltpu.VMEM((members, *w_group_t.shape), BF)]
        + [pltpu.VMEM((full[0] // 128, n, 128), BF)] * 4,
        compiler_params=params(44),
        cost_estimate=cost(14 * 10**9, 12 << 20, 7 * 10**6),
        name="group",
    )(
        core, rows, gain, group_col,
        *map(in_hbm, (w_group_t, w_gate_t, w_out, *pieces)),
    )


def join_kernel(me_ref, t0_ref, t1_ref, t2_ref, t3_ref, g_ref, o_ref, tmp):
    me = me_ref[0]
    for c in range(tmp.shape[0]):
        tmp[c] = g_ref[:, c * 128 : (c + 1) * 128].astype(F32)
    for distance, t_ref in zip(DISTANCES, (t0_ref, t1_ref, t2_ref, t3_ref)):
        m = lax.rem(me + 4 - distance, 4)
        for a in range(2):
            for j in range(2):
                rows = [
                    tmp[c, pl.ds(j * 8 + m * 2 + a, 128, stride=16), :].T
                    for c in range(tmp.shape[0])
                ]
                at = slice(j * 128, (j + 1) * 128)
                for e in range(2):
                    i = 2 * e + a
                    o_ref[m * 4 + i, :128, at] = (
                        t_ref[i, :128, at].astype(F32) + rows[e]
                    ).astype(BF)
                    o_ref[m * 4 + i, 128:, at] = (
                        t_ref[i, 128:, at].astype(F32) + rows[2][e * 64 : (e + 1) * 64]
                    ).astype(BF)


def join(me, pieces, group):
    part, cols, patches = pieces[0].shape
    vmem = pl.BlockSpec(memory_space=pltpu.VMEM)
    return pl.pallas_call(
        join_kernel,
        out_shape=jax.ShapeDtypeStruct((4 * part, cols, patches), BF),
        in_specs=[pl.BlockSpec(memory_space=pltpu.SMEM)] + [vmem] * 5,
        out_specs=vmem,
        scratch_shapes=[pltpu.VMEM((group.shape[1] // 128, group.shape[0], 128), F32)],
        compiler_params=params(20),
        cost_estimate=cost(0, 8 << 20),
        name="join",
    )(me, *pieces, group)


def after(value, *others):
    return lax.optimization_barrier((value, *others))[0]


def shift(value, by):
    n = lax.axis_size("mp")
    return lax.ppermute(value, "mp", [(i, (i + by) % n) for i in range(n)])


def swap(value):
    return lax.ppermute(value, "core", [(0, 1), (1, 0)])


def per_device(series_in, norm_gain, w_time, w_group, w_gate, w_out, group_of):
    ser, patches, width = series_in.shape
    members = lax.axis_size("mp")
    n_ser = lax.axis_size("sc") * lax.axis_size("core")
    chan = w_gate.shape[1]
    me = lax.axis_index("mp").reshape(1)
    core = lax.axis_index("core").reshape(1)
    gain = norm_gain.reshape(1, width)
    w_time_t = jnp.transpose(w_time, (1, 2, 0)).reshape(3 * chan, width)
    w_group_t = jnp.transpose(w_group, (1, 2, 0)).reshape(3 * chan, width)
    w_gate_t = w_gate.T

    half = half_weights(core, w_group_t, w_gate_t, w_out)
    below = shift(half, 1)
    above = shift(half, 3)
    packed = pack(after(series_in, half), me, n_ser)
    spread = lax.all_to_all(
        packed.reshape(n_ser, ser, 2 * width), SERIES_AXES, 0, 0, tiled=True
    ).reshape(n_ser * ser, 2 * width)

    sent_group = group_of.reshape(n_ser, members, 2, 2).transpose(0, 2, 1, 3).reshape(-1, 1)
    quarter = half.shape[0] // 2
    x = after(series_in, packed, sent_group)
    part = ser // 2
    times = time_part(x, gain, w_time_t, None, 0, part)
    far_a = shift(after(below[:quarter], times), 1)
    far_b = shift(after(above[quarter:], times), 3)
    near = [swap(after(below, times)), swap(after(above, times))]
    times = time_part(x, gain, w_time_t, after(times, *near), part, ser)
    far = [swap(after(far_a, times)), swap(after(far_b, times))]
    pieces = [below, above, far_a, far_b, *near, *far]
    back, out_w = group_part(
        core, spread, gain, sent_group, after(w_group_t, times), w_gate_t, w_out, pieces, members
    )
    times = lax.all_to_all(times, "mp", 0, 0, tiled=True)
    back, times = lax.optimization_barrier((back, times))
    back = back.reshape(members * n_ser, 16, 2 * chan)
    back = lax.all_to_all(back, ("mp", *SERIES_AXES), 0, 0, tiled=True)

    cols = project(me, times.reshape(members, ser // members, chan, patches), out_w)
    farthest = shift(cols[3], 2)
    cols = [cols[0], shift(cols[1], 1), shift(cols[2], 3), farthest]
    out = join(me, cols, back.reshape(members * n_ser * 16, 2 * chan))
    return jnp.transpose(out, (0, 2, 1))


def solution(mesh):
    n_ser, n_mp = mesh.devices.shape
    split = Mesh(mesh.devices.reshape(n_ser // 2, 2, n_mp), ("sc", "core", "mp"))
    placed = (
        P(SERIES_AXES, None, None),
        P(),
        P(None, "mp", None),
        P(None, "mp", None),
        P(None, "mp"),
        P("mp", None),
        P(),
    )
    return jax.shard_map(
        per_device,
        mesh=split,
        in_specs=placed,
        out_specs=P(SERIES_AXES, None, "mp"),
        check_vma=False,
    )
```

```python
from functools import partial

import jax
import jax.numpy as jnp
from jax import lax
from jax.experimental import pallas as pl
from jax.experimental.pallas import tpu as pltpu
from jax.sharding import Mesh
from jax.sharding import PartitionSpec as P

BF = jnp.bfloat16
F32 = jnp.float32
SERIES_AXES = ("sc", "core")
BIG = 2.0**50
DISTANCES = (0, 1, 3, 2)


def nt(a, b):
    return lax.dot_general(a, b, (((1,), (1,)), ((), ())), preferred_element_type=F32)


def nn(a, b):
    return lax.dot_general(a, b, (((1,), (0,)), ((), ())), preferred_element_type=F32)


def tn(a, b):
    return lax.dot_general(a, b, (((0,), (0,)), ((), ())), preferred_element_type=F32)


def cost(flops, moved, exps=0):
    return pl.CostEstimate(flops=flops, bytes_accessed=moved, transcendentals=exps)


def in_hbm(x):
    return pltpu.with_memory_space_constraint(x, pltpu.HBM)


def params(mib):
    return pltpu.CompilerParams(vmem_limit_bytes=mib << 20)


def normed_rows(x, gain):
    xf = x.astype(F32)
    mean_sq = jnp.mean(xf * xf, axis=-1, keepdims=True)
    return (xf * lax.rsqrt(mean_sq + 1e-06) * gain).astype(BF)


def half_kernel(core_ref, group_ref, gate_ref, out_ref, o_ref):
    at = 0
    for ref in (group_ref, gate_ref, out_ref):
        rows = ref.shape[0]
        o_ref[at : at + rows] = ref[...]
        at += rows


def half_weights(core, w_group_t, w_gate_t, w_out):
    weights = (w_group_t, w_gate_t, w_out)
    width = w_out.shape[1]
    rows = sum(w.shape[0] for w in weights) // 2
    return pl.pallas_call(
        half_kernel,
        out_shape=pltpu.HBM((rows, width), BF),
        grid_spec=pltpu.PrefetchScalarGridSpec(
            num_scalar_prefetch=1,
            grid=(1,),
            in_specs=[
                pl.BlockSpec((w.shape[0] // 2, width), lambda i, core: (core[0], 0))
                for w in weights
            ],
            out_specs=pl.BlockSpec((rows, width), lambda i, core: (0, 0)),
        ),
        compiler_params=params(16),
        cost_estimate=cost(0, 2 << 20),
        name="half",
    )(core, *map(in_hbm, weights))


def place(i):
    return (i // 2 % 2) * 8 + (i // 4) * 2 + i % 2


def pack_kernel(me_ref, x_ref, o_ref, tmp):
    ser, rows, _ = x_ref.shape
    blocks = tmp.shape[0]
    for i in range(ser):
        values = x_ref[i].astype(F32)
        for c in range(blocks):
            tmp[c, pl.ds(place(i), rows, stride=ser), :] = values[:, c * 128 : (c + 1) * 128]
    for c in range(blocks):
        o_ref[:, c * 128 : (c + 1) * 128] = tmp[c].astype(BF)


def pack(series_in, me, n_ser):
    ser, patches, width = series_in.shape
    n_mp = patches // (2 * n_ser)
    return pl.pallas_call(
        pack_kernel,
        out_shape=jax.ShapeDtypeStruct((n_ser * ser, 2 * width), BF),
        grid_spec=pltpu.PrefetchScalarGridSpec(
            num_scalar_prefetch=1,
            grid=(2,),
            in_specs=[pl.BlockSpec((ser, n_ser, width), lambda j, me: (0, j * n_mp + me[0], 0))],
            out_specs=pl.BlockSpec((n_ser * ser, width), lambda j, me: (0, j)),
            scratch_shapes=[pltpu.VMEM((width // 128, n_ser * ser, 128), F32)],
        ),
        compiler_params=params(16),
        cost_estimate=cost(0, 4 << 20),
        name="pack",
    )(me, in_hbm(series_in))


def time_kernel(x_ref, gain_ref, w_ref, buf_ref, o_ref, w_q, w_k, w_v):
    hd = 64
    heads = w_ref.shape[0] // (3 * hd)

    @pl.when(pl.program_id(0) == 0)
    def _():
        for h in range(heads):
            base = h * 3 * hd
            w_q[h * hd : (h + 1) * hd] = w_ref[base : base + hd]
            w_k[h * hd : (h + 1) * hd] = w_ref[base + hd : base + 2 * hd]
            w_v[h * hd : (h + 1) * hd] = w_ref[base + 2 * hd : base + 3 * hd]
        for w in (w_q, w_k, w_v):
            w[heads * hd :] = jnp.zeros((hd, w.shape[1]), BF)

    ser, rows, width = x_ref.shape
    normed = normed_rows(x_ref[...].reshape(ser * rows, width), gain_ref[...])
    queries = (nt(normed, w_q[...]) * 0.125).astype(BF)
    keys = nt(normed, w_k[...]).astype(BF)
    values = nt(normed, w_v[...]).astype(BF)
    lower = lax.broadcasted_iota(jnp.int32, (rows, 128), 1) < hd
    for i in range(ser):
        span = slice(i * rows, (i + 1) * rows)
        for b in range((heads + 1) // 2):
            at = slice(b * 128, (b + 1) * 128)
            q_b, k_b, v_b = queries[span, at], keys[span, at], values[span, at]
            outs = []
            for e in range(min(2, heads - 2 * b)):
                own = lower if e == 0 else ~lower
                k_e = jnp.where(own, k_b, jnp.zeros_like(k_b))
                v_e = jnp.where(own, v_b, jnp.ones_like(v_b))
                scores = nt(q_b, k_e)
                top = jnp.max(scores, axis=1, keepdims=True)
                outs.append(nn(jnp.exp(scores - top).astype(BF), v_e))
            if len(outs) == 2:
                num = jnp.where(lower, outs[0], outs[1])
                den = pltpu.roll(jnp.where(lower, outs[1], outs[0]), 64, 1)
            else:
                num, den = outs[0], pltpu.roll(outs[0], 64, 1)
            out = (num / den).T.astype(BF)
            if len(outs) == 2:
                o_ref[i, at] = out
            else:
                o_ref[i, b * 128 : b * 128 + hd] = out[:hd]


def time_part(series_in, gain, w_time_t, buffer, first, last, step=4):
    ser, patches, width = series_in.shape
    chan = w_time_t.shape[0] // 3
    out = pltpu.HBM((ser, chan, patches), BF)
    base = first // step
    args = (in_hbm(series_in), gain, in_hbm(w_time_t)) + (() if buffer is None else (in_hbm(buffer),))

    def kernel(x_ref, gain_ref, w_ref, *refs):
        time_kernel(x_ref, gain_ref, w_ref, None, *refs[len(args) - 3 :])

    return pl.pallas_call(
        kernel,
        out_shape=out,
        grid=((last - first) // step,),
        in_specs=[
            pl.BlockSpec((step, patches, width), lambda i: (base + i, 0, 0)),
            pl.BlockSpec((1, width), lambda i: (0, 0)),
            pl.BlockSpec((3 * chan, width), lambda i: (0, 0)),
        ]
        + [pl.BlockSpec(memory_space=pl.ANY)] * (len(args) - 3),
        out_specs=pl.BlockSpec((step, chan, patches), lambda i: (base + i, 0, 0)),
        scratch_shapes=[pltpu.VMEM((chan + 64, width), BF)] * 3,
        input_output_aliases={} if buffer is None else {3: 0},
        compiler_params=params(20),
        cost_estimate=cost(10**8, 1 << 18),
        name="time",
    )(*args)


def gather_weights(core, group_ref, gate_ref, out_ref, pieces, w_q, w_k, w_v, w_gate, w_out, wg):
    hd = 64
    half_g, half_o = group_ref.shape[0] // 2, out_ref.shape[0] // 2
    chan = 2 * half_o
    w_gate[:chan] = gate_ref[...]
    w_out[:chan] = out_ref[...]
    wg[0] = group_ref[...]
    for k in range(2):
        which = core if k == 0 else 1 - core
        at_g = pl.multiple_of(which * half_g, 16)
        at_o = pl.multiple_of(which * half_o, 16)
        for r in (1, 2, 3):
            ref = pieces[4 * k + r - 1]
            first = ref.shape[0] if r == 3 else half_g
            wg[r, pl.ds(at_g, first), :] = ref[:first]
            skip = first
            if r == 3:
                ref = pieces[4 * k + 3]
                skip = half_g - first
                wg[r, pl.ds(at_g + first, skip), :] = ref[:skip]
            w_gate[pl.ds(r * chan + at_o, half_o), :] = ref[skip : skip + half_o]
            w_out[pl.ds(r * chan + at_o, half_o), :] = ref[skip + half_o : skip + 2 * half_o]
    heads_m = group_ref.shape[0] // (3 * hd)
    for h in range(4 * heads_m):
        m, base = h // heads_m, (h % heads_m) * 3 * hd
        w_q[h * hd : (h + 1) * hd] = wg[m, base : base + hd]
        w_k[h * hd : (h + 1) * hd] = wg[m, base + hd : base + 2 * hd]
        w_v[h * hd : (h + 1) * hd] = wg[m, base + 2 * hd : base + 3 * hd]


def project_kernel(distances, me_ref, t_ref, w_ref, *refs):
    *outs, w_t = refs
    members, ser, chan, patches = t_ref.shape

    @pl.when(pl.program_id(0) == 0)
    def _():
        w_t[...] = w_ref[...].T

    me = me_ref[0]
    for i in range(ser):
        rows = jnp.concatenate(
            [t_ref[lax.rem(me + 4 - distance, 4), i] for distance in DISTANCES], axis=0
        )
        for distance, o_ref in zip(distances, outs):
            at = pl.multiple_of(lax.rem(me + distance, 4) * chan, 16)
            o_ref[i] = nn(w_t[pl.ds(at, chan), :], rows).astype(BF)


def project(me, pieces, w_out, distances):
    members, ser, chan, patches = pieces.shape
    spec = pl.BlockSpec((2, chan, patches), lambda i, me: (i, 0, 0))
    return pl.pallas_call(
        partial(project_kernel, distances),
        out_shape=(jax.ShapeDtypeStruct(pieces.shape[1:], BF),) * len(distances),
        grid_spec=pltpu.PrefetchScalarGridSpec(
            num_scalar_prefetch=1,
            grid=(ser // 2,),
            in_specs=[
                pl.BlockSpec((members, 2, chan, patches), lambda i, me: (0, i, 0, 0)),
                pl.BlockSpec(w_out.shape, lambda i, me: (0, 0)),
            ],
            out_specs=[spec] * len(distances),
            scratch_shapes=[pltpu.VMEM(w_out.shape, BF)],
        ),
        compiler_params=params(16),
        cost_estimate=cost(12 * 10**8, 4 << 20),
        name="project",
    )(me, pieces, in_hbm(w_out))


def group_kernel(core_ref, x_ref, gain_ref, gcol_ref, group_ref, gate_ref, out_ref, *refs):
    pieces = refs[:8]
    o_ref, wout_ref, wq_ref, wk_ref, wv_ref, wgate_ref, wg, kmat, qmat, vmat, gated = refs[8:]
    gather_weights(core_ref[0], group_ref, gate_ref, out_ref, pieces,
                   wq_ref, wk_ref, wv_ref, wgate_ref, wout_ref, wg)
    n = x_ref.shape[0]
    width = wq_ref.shape[1]
    blocks = kmat.shape[0]
    members = o_ref.shape[0]
    lanes = lax.broadcasted_iota(jnp.int32, (n, 128), 1)
    same = gcol_ref[...] == lanes
    k_mask = jnp.where(same, 0.0, -BIG).astype(BF)
    q_mask = jnp.where(same, BIG, 0.0).astype(BF)
    lower = lanes < 64
    for j in range(2):
        normed = normed_rows(x_ref[:, j * width : (j + 1) * width], gain_ref[...])
        queries = (nt(normed, wq_ref[...]) * 0.125).astype(BF)
        keys = nt(normed, wk_ref[...]).astype(BF)
        values = nt(normed, wv_ref[...]).astype(BF)
        for b in range(blocks):
            at = slice(b * 128, (b + 1) * 128)
            qmat[b] = queries[:, at]
            kmat[b] = keys[:, at]
            vmat[b] = values[:, at]

        for b in range(blocks):
            q_b = jnp.concatenate([qmat[b], q_mask], axis=1)
            k_b, v_b = kmat[b], vmat[b]
            outs = []
            for e in range(2):
                own = lower if e == 0 else ~lower
                k_e = jnp.concatenate([jnp.where(own, k_b, jnp.zeros_like(k_b)), k_mask], axis=1)
                v_e = jnp.where(own, v_b, jnp.ones_like(v_b))
                scores = nt(q_b, k_e)
                top = jnp.max(scores, axis=1, keepdims=True)
                outs.append(nn(jnp.exp(scores - top).astype(BF), v_e))
            num = jnp.where(lower, outs[0], outs[1])
            den = pltpu.roll(jnp.where(lower, outs[1], outs[0]), 64, 1)
            gated[b] = (num / den).astype(BF)

        gate = jax.nn.sigmoid(nt(normed, wgate_ref[...]))
        rows = jnp.concatenate(
            [
                (gate[:, b * 128 : (b + 1) * 128] * gated[b].astype(F32)).astype(BF)
                for b in range(blocks)
            ],
            axis=1,
        )
        out = nn(rows, wout_ref[...])
        cols = width // members
        for m in range(members):
            part = out[:, m * cols : (m + 1) * cols].reshape(n // 16, 16, cols)
            low, high = part[:, :8], part[:, 8:]
            o_ref[m, :, j * 8 : (j + 1) * 8] = jnp.concatenate(
                [low[:, :, :128], high[:, :, :128], low[:, :, 128:], high[:, :, 128:]], axis=-1
            ).astype(BF)


def group_part(core, rows, gain, group_col, w_group_t, w_gate_t, w_out, pieces, members):
    n = rows.shape[0]
    chan, width = w_out.shape
    full = (members * chan, width)
    vmem = pl.BlockSpec(memory_space=pltpu.VMEM)
    return pl.pallas_call(
        group_kernel,
        out_shape=(
            pltpu.HBM((members, n // 16, 16, 2 * width // members), BF),
            pltpu.HBM(full, BF),
        ),
        in_specs=[pl.BlockSpec(memory_space=pltpu.SMEM)] + [vmem] * (6 + len(pieces)),
        out_specs=(vmem, vmem),
        scratch_shapes=[pltpu.VMEM(full, BF)] * 4
        + [pltpu.VMEM((members, *w_group_t.shape), BF)]
        + [pltpu.VMEM((full[0] // 128, n, 128), BF)] * 4,
        compiler_params=params(44),
        cost_estimate=cost(14 * 10**9, 12 << 20, 7 * 10**6),
        name="group",
    )(
        core, rows, gain, group_col,
        *map(in_hbm, (w_group_t, w_gate_t, w_out, *pieces)),
    )


def join_kernel(me_ref, t0_ref, t1_ref, t2_ref, t3_ref, g_ref, o_ref, tmp):
    me = me_ref[0]
    for c in range(tmp.shape[0]):
        tmp[c] = g_ref[:, c * 128 : (c + 1) * 128].astype(F32)
    for distance, t_ref in zip(DISTANCES, (t0_ref, t1_ref, t2_ref, t3_ref)):
        m = lax.rem(me + 4 - distance, 4)
        for a in range(2):
            for j in range(2):
                rows = [
                    tmp[c, pl.ds(j * 8 + m * 2 + a, 128, stride=16), :].T
                    for c in range(tmp.shape[0])
                ]
                at = slice(j * 128, (j + 1) * 128)
                for e in range(2):
                    i = 2 * e + a
                    o_ref[m * 4 + i, :128, at] = (
                        t_ref[i, :128, at].astype(F32) + rows[e]
                    ).astype(BF)
                    o_ref[m * 4 + i, 128:, at] = (
                        t_ref[i, 128:, at].astype(F32) + rows[2][e * 64 : (e + 1) * 64]
                    ).astype(BF)


def join(me, pieces, group):
    part, cols, patches = pieces[0].shape
    vmem = pl.BlockSpec(memory_space=pltpu.VMEM)
    return pl.pallas_call(
        join_kernel,
        out_shape=jax.ShapeDtypeStruct((4 * part, cols, patches), BF),
        in_specs=[pl.BlockSpec(memory_space=pltpu.SMEM)] + [vmem] * 5,
        out_specs=vmem,
        scratch_shapes=[pltpu.VMEM((group.shape[1] // 128, group.shape[0], 128), F32)],
        compiler_params=params(20),
        cost_estimate=cost(0, 8 << 20),
        name="join",
    )(me, *pieces, group)


def after(value, *others):
    return lax.optimization_barrier((value, *others))[0]


def shift(value, by):
    n = lax.axis_size("mp")
    return lax.ppermute(value, "mp", [(i, (i + by) % n) for i in range(n)])


def swap(value):
    return lax.ppermute(value, "core", [(0, 1), (1, 0)])


def per_device(series_in, norm_gain, w_time, w_group, w_gate, w_out, group_of):
    ser, patches, width = series_in.shape
    members = lax.axis_size("mp")
    n_ser = lax.axis_size("sc") * lax.axis_size("core")
    chan = w_gate.shape[1]
    me = lax.axis_index("mp").reshape(1)
    core = lax.axis_index("core").reshape(1)
    gain = norm_gain.reshape(1, width)
    w_time_t = jnp.transpose(w_time, (1, 2, 0)).reshape(3 * chan, width)
    w_group_t = jnp.transpose(w_group, (1, 2, 0)).reshape(3 * chan, width)
    w_gate_t = w_gate.T

    half = half_weights(core, w_group_t, w_gate_t, w_out)
    below = shift(half, 1)
    above = shift(half, 3)
    packed = pack(after(series_in, half), me, n_ser)
    spread = lax.all_to_all(
        packed.reshape(n_ser, ser, 2 * width), SERIES_AXES, 0, 0, tiled=True
    ).reshape(n_ser * ser, 2 * width)

    sent_group = group_of.reshape(n_ser, members, 2, 2).transpose(0, 2, 1, 3).reshape(-1, 1)
    quarter = half.shape[0] // 2
    x = after(series_in, packed, sent_group)
    part = ser // 2
    times = time_part(x, gain, w_time_t, None, 0, part)
    far_a = shift(after(below[:quarter], times), 1)
    far_b = shift(after(above[quarter:], times), 3)
    near = [swap(after(below, times)), swap(after(above, times))]
    times = time_part(x, gain, w_time_t, after(times, *near), part, ser)
    far = [swap(after(far_a, times)), swap(after(far_b, times))]
    pieces = [below, above, far_a, far_b, *near, *far]
    back, out_w = group_part(
        core, spread, gain, sent_group, after(w_group_t, times), w_gate_t, w_out, pieces, members
    )
    times = lax.all_to_all(times, "mp", 0, 0, tiled=True)
    back, times = lax.optimization_barrier((back, times))
    back = back.reshape(members * n_ser, 16, 2 * chan)
    back = lax.all_to_all(back, ("mp", *SERIES_AXES), 0, 0, tiled=True)

    times = times.reshape(members, ser // members, chan, patches)
    (two,) = project(me, times, out_w, (2,))
    own, one, three = project(me, after(times, two), out_w, (0, 1, 3))
    cols = [own, shift(one, 1), shift(three, 3), shift(two, 2)]
    out = join(me, cols, back.reshape(members * n_ser * 16, 2 * chan))
    return jnp.transpose(out, (0, 2, 1))


def solution(mesh):
    n_ser, n_mp = mesh.devices.shape
    split = Mesh(mesh.devices.reshape(n_ser // 2, 2, n_mp), ("sc", "core", "mp"))
    placed = (
        P(SERIES_AXES, None, None),
        P(),
        P(None, "mp", None),
        P(None, "mp", None),
        P(None, "mp"),
        P("mp", None),
        P(),
    )
    return jax.shard_map(
        per_device,
        mesh=split,
        in_specs=placed,
        out_specs=P(SERIES_AXES, None, "mp"),
        check_vma=False,
    )
```
